512 devices in a mesh: dom: 64 (over y, z_lo, core), cls: 8 (over z_hi, x).
Axes of the slice: x: 4, y: 4, z: 16 (z_hi: 2, z_lo: 8; z = z_hi * 8 + z_lo), core: 2. Of those that a mesh axis runs over, the one named last changes fastest.
Arguments:
- particles: bfloat16 [36864, 4096], P('dom'), may hold values from -6 to 6
- shift_index: int32 [36864], P('dom'), may hold values from 0 to 24
- prev_class: int32 [36864], P('dom'), may hold values from 0 to 63
- prev_rotation: int32 [36864], P('dom'), may hold values from 0 to 23
- precision: float32 [36864], P('dom'), may hold values from 0.25 to 300
- references: bfloat16 [64, 98304], P('cls', 'dom')
Outputs:
- new_references: float32 [64, 98304], P('cls', 'dom')
- log_evidence: float32 [36864], P('dom')
The draws below stay inside these ranges and needn't reach their ends.
All inputs are finite; a program needn't handle non-finite values.
Results may differ from the reference program's by a relative error of at most 0.0039.
Values may be sent and summed in bfloat16 or wider, within the bound.
No kernel may reach another device: no remote copies, remote signals or barrier semaphores. Data moves between devices by JAX's collectives and lax.ppermute only.
A program may use at most 64 MiB of HBM per device.

```python
import math
import jax
import jax.numpy as jnp
from jax import lax

BOX = 64
F = 4096
R = 24
CLASSES = 64
P_DEV = 576
PARTICLES = 36864


def draw_precision(key, part):
    uniform_part = jax.random.uniform(key, (PARTICLES,), jnp.float32)
    lowest, highest = (0.25, 2.0)
    return jnp.exp(jnp.log(lowest) + uniform_part * (jnp.log(highest) - jnp.log(lowest)))


def draw_references(key, part):
    row_key = jax.random.fold_in(key, 11)
    random_entry_key = jax.random.fold_in(key, 23)
    row_scale = jnp.exp(jax.random.uniform(row_key, (CLASSES * R, 1), jnp.float32, jnp.log(0.4), jnp.log(4.0)))
    entries = jnp.clip(jax.random.normal(random_entry_key, (CLASSES * R, F), jnp.float32), -4.0, 4.0)
    return (entries * row_scale / BOX).reshape(CLASSES, R * F).astype(jnp.bfloat16)


def plant(drawn, stream_key, smallest, largest):
    longest = drawn.shape.index(max(drawn.shape))
    spots = []
    for shift in (0, 1):
        where = [jax.random.randint(jax.random.fold_in(stream_key, axis), (), 0, length) for axis, length in enumerate(drawn.shape)]
        where[longest] = (where[longest] + shift) % drawn.shape[longest]
        spots.append(tuple(where))
    return drawn.at[spots[0]].set(smallest).at[spots[1]].set(largest)


def level_of(rng, dims, split, smallest, top_value):
    loudness = 1.0
    for axis_at, shards_of in split:
        steps = jax.random.uniform(jax.random.fold_in(jax.random.fold_in(rng, 6), axis_at), (shards_of,), jnp.float32, smallest / len(split), top_value / len(split))
        loudness = loudness * jnp.repeat(jnp.exp(steps), dims[axis_at] // shards_of).reshape((-1,) + (1,) * (len(dims) - 1 - axis_at))
    return loudness


def centred(key, extent, width, most, cuts=(), kind=jnp.bfloat16):
    gain = level_of(key, extent, cuts, -0.22, 0.18) if cuts else 1.0
    drawn = jax.random.normal(key, extent, jnp.float32) * width * gain
    return jnp.minimum(jnp.maximum(drawn, -most), most).astype(kind)


def setup_inputs(seed: int = 0) -> dict:
    splits = jax.random.split(jax.random.key(seed), 7)
    return {
        "particles": centred(splits[0], (PARTICLES, F), 1.0, 6.0, ((0, 64),)),
        "shift_index": plant(jax.random.randint(splits[1], (PARTICLES,), 0, 25), jax.random.fold_in(splits[1], 1), 0, 24).astype(jnp.int32),
        "prev_class": plant(jax.random.randint(splits[2], (PARTICLES,), 0, CLASSES), jax.random.fold_in(splits[2], 1), 0, CLASSES - 1).astype(jnp.int32),
        "prev_rotation": plant(jax.random.randint(splits[3], (PARTICLES,), 0, R), jax.random.fold_in(splits[3], 1), 0, R - 1).astype(jnp.int32),
        "precision": draw_precision(jax.random.fold_in(splits[6], 71), 0),
        "references": draw_references(jax.random.fold_in(splits[6], 71), 0),
    }


two_pi = 2.0 * math.pi
shift_side = 5
class_reward = 1.0
prior_mass = 1.0


def shift_particles(particles, shift_index, box_side):
    half_width = particles.shape[1] // 2
    frequency = jnp.arange(half_width, dtype=jnp.int32)
    freq_x = frequency % box_side - box_side // 2
    freq_y = frequency // box_side
    step_x = shift_index % shift_side - 2
    step_y = shift_index // shift_side - 2
    phase_int = (freq_x[None, :] * step_x[:, None] + freq_y[None, :] * step_y[:, None]) % box_side
    phase_angle = phase_int.astype(jnp.float32) * (two_pi / box_side)
    cosine_values = jnp.cos(phase_angle)
    sine_values = jnp.sin(phase_angle)
    real_part = particles[:, :half_width].astype(jnp.float32)
    imag_part = particles[:, half_width:].astype(jnp.float32)
    out_real = real_part * cosine_values + imag_part * sine_values
    out_imag = imag_part * cosine_values - real_part * sine_values
    return jnp.concatenate([out_real, out_imag], axis=1).astype(jnp.bfloat16)


def prior_term(prev_class, prev_rotation, class_ids, rotation_ids, rotations):
    rotation_distance = jnp.abs(rotation_ids[None, :] - prev_rotation[:, None])
    rotation_distance = jnp.minimum(rotation_distance, rotations - rotation_distance).astype(jnp.float32)
    prior_spread_width = rotations / 8.0
    match_flags = (class_ids[None, :] == prev_class[:, None]).astype(jnp.float32)
    return -rotation_distance * rotation_distance / (2.0 * prior_spread_width * prior_spread_width) + class_reward * match_flags


def reference(particles, shift_index, prev_class, prev_rotation, precision, references):
    flat_table = references.reshape(CLASSES * R, F)
    half_norm = 0.5 * jnp.sum(jnp.square(flat_table.astype(jnp.float32)), axis=1)
    candidate = jnp.arange(CLASSES * R, dtype=jnp.int32)
    class_ids = candidate // R
    rotation_ids = candidate % R
    blocks = PARTICLES // P_DEV

    def one_block(carry, block):
        numerator, denominator = carry
        part_block, shift_block, class_block, rotation_block, precision_block = block
        shifted = shift_particles(part_block, shift_block, BOX)
        correlation = lax.dot_general(shifted, flat_table, (((1,), (1,)), ((), ())), preferred_element_type=jnp.float32)
        scores = precision_block[:, None] * (correlation - half_norm[None, :])
        scores = scores + prior_term(class_block, rotation_block, class_ids, rotation_ids, R)
        top_score = jnp.max(scores, axis=1, keepdims=True)
        exponent = jnp.exp(scores - top_score)
        total_mass = jnp.sum(exponent, axis=1, keepdims=True)
        probs = exponent / total_mass
        weights = probs.astype(jnp.bfloat16)
        numerator = numerator + lax.dot_general(weights, shifted, (((0,), (0,)), ((), ())), preferred_element_type=jnp.float32)
        denominator = denominator + jnp.sum(probs, axis=0)
        evidence = (top_score + jnp.log(total_mass))[:, 0]
        return (numerator, denominator), evidence

    start_sums = (jnp.zeros((CLASSES * R, F), jnp.float32), jnp.zeros((CLASSES * R,), jnp.float32))
    blocked = (particles.reshape(blocks, P_DEV, F), shift_index.reshape(blocks, P_DEV),
               prev_class.reshape(blocks, P_DEV), prev_rotation.reshape(blocks, P_DEV),
               precision.reshape(blocks, P_DEV))
    (numerator, denominator), evidence = lax.scan(one_block, start_sums, blocked)
    refreshed_references = numerator / (denominator[:, None] + prior_mass)
    return refreshed_references.reshape(CLASSES, R * F), evidence.reshape(PARTICLES)
```

```python
import math

import jax
import jax.numpy as jnp
from jax import lax
from jax.experimental import pallas as pl
from jax.experimental.pallas import tpu as pltpu
from jax.sharding import Mesh
from jax.sharding import PartitionSpec as P

BOX = 64
F = 4096
H = F // 2
R = 24
K = 8
ROWS = K * R
SHIFTS = 25
SIDE = 5
P_DEV = 576
ROW_BLOCK = 96
TILES = 12

bf16 = jnp.bfloat16
f32 = jnp.float32

Z = ("za", "zb")
CLS = ("zh", "x")
DOM = ("y", "za", "zb", "c")


def phase_table():
    frequency = jnp.arange(H, dtype=jnp.int32)
    freq_x = frequency % BOX - BOX // 2
    freq_y = frequency // BOX
    shift = jnp.arange(SHIFTS, dtype=jnp.int32)
    step_x = shift % SIDE - 2
    step_y = shift // SIDE - 2
    phase = (freq_x[None, :] * step_x[:, None] + freq_y[None, :] * step_y[:, None]) % BOX
    angle = phase.astype(f32) * (2.0 * math.pi / BOX)
    exact = jnp.concatenate([jnp.cos(angle), jnp.sin(angle)], axis=1)
    high = lax.reduce_precision(exact, 8, 7)
    rest = exact - high
    middle = lax.reduce_precision(rest, 8, 7)
    low = rest - middle
    return jnp.concatenate([high, middle, low, jnp.zeros((128 - 3 * SHIFTS, F), f32)], axis=0).astype(bf16)


def shift_kernel(index_ref, table_ref, image_ref, out_ref):
    index = index_ref[...]
    lane = lax.broadcasted_iota(jnp.int32, (ROW_BLOCK, 128), 1)
    chosen = (lane == index) | (lane == index + SHIFTS) | (lane == index + 2 * SHIFTS)
    chosen = jnp.where(chosen, 1.0, 0.0).astype(bf16)
    for at in range(0, H, 512):
        cosine = jnp.dot(chosen, table_ref[:, at : at + 512], preferred_element_type=f32)
        sine = jnp.dot(chosen, table_ref[:, H + at : H + at + 512], preferred_element_type=f32)
        real = image_ref[:, at : at + 512].astype(f32)
        imag = image_ref[:, H + at : H + at + 512].astype(f32)
        out_ref[:, at : at + 512] = (real * cosine + imag * sine).astype(bf16)
        out_ref[:, H + at : H + at + 512] = (imag * cosine - real * sine).astype(bf16)


def shift_particles(particles, shift_index):
    return pl.pallas_call(
        shift_kernel,
        grid=(P_DEV // ROW_BLOCK,),
        in_specs=[
            pl.BlockSpec((ROW_BLOCK, 1), lambda i: (i, 0)),
            pl.BlockSpec((128, F), lambda i: (0, 0)),
            pl.BlockSpec((ROW_BLOCK, F), lambda i: (i, 0)),
        ],
        out_specs=pl.BlockSpec((ROW_BLOCK, F), lambda i: (i, 0)),
        out_shape=jax.ShapeDtypeStruct((P_DEV, F), bf16),
        compiler_params=pltpu.CompilerParams(vmem_limit_bytes=24 << 20),
        name="shift",
    )(shift_index[:, None], phase_table(), particles)


def exchange(array, axis):
    return lax.all_to_all(array, axis, 0, 0, tiled=True)


def gather_table(references):
    mine = references.reshape(K, TILES, 128).transpose(1, 0, 2)
    along_z = exchange(jnp.broadcast_to(mine, (8, TILES, K, 128)), Z)
    along_y = exchange(jnp.broadcast_to(along_z, (4, 8, TILES, K, 128)), "y")
    both = lax.all_gather(along_y, "c", axis=0)
    both = both.reshape(2, 4, 2, 4, TILES, K, 128)
    both = both.transpose(1, 2, 3, 0, 4, 5, 6).reshape(8, 3, 32, K, 128)
    return both.transpose(0, 1, 3, 2, 4).reshape(ROWS, F)


def scatter_sums(numerator, occupancy):
    pieces = numerator.reshape(8, 3, K, 32, 128).transpose(0, 1, 3, 2, 4)
    pieces = pieces.reshape(4, 2, 4, 2, TILES, K, 128).transpose(3, 0, 1, 2, 4, 5, 6)
    spread = jnp.broadcast_to(occupancy.reshape(8, 3, 1, K), (8, 3, 8, K))
    spread = spread.reshape(4, 2, 4, 2, 3, K).transpose(3, 0, 1, 2, 5, 4)
    high = lax.reduce_precision(spread, 8, 7)
    extra = jnp.concatenate([high, spread - high, jnp.zeros((2, 4, 2, 4, K, 122), f32)], axis=-1)
    pieces = jnp.concatenate([pieces, extra[:, :, :, :, None]], axis=4).astype(bf16)
    pieces = exchange(pieces, "c").astype(f32)
    pieces = jnp.sum(pieces, axis=0).astype(bf16)
    pieces = exchange(pieces, "y").astype(f32)
    pieces = jnp.sum(pieces, axis=0).astype(bf16)
    pieces = pieces.reshape(8, TILES + 1, K, 128)
    pieces = exchange(pieces, Z).astype(f32)
    pieces = jnp.sum(pieces, axis=0)
    summed = pieces[:TILES].reshape(3, 4, K, 128).transpose(2, 0, 1, 3)
    mass = pieces[TILES, :, 0:3] + pieces[TILES, :, 3:6]
    return summed, mass


def on_device(particles, shift_index, prev_class, prev_rotation, precision, references):
    table = gather_table(references)
    shifted = shift_particles(particles, shift_index)
    half_norm = 0.5 * jnp.sum(jnp.square(table.astype(f32)), axis=1)
    row = jnp.arange(ROWS, dtype=jnp.int32)
    class_ids = lax.axis_index(CLS) * K + row % K
    rotation_ids = row // K
    correlation = lax.dot_general(table, shifted, (((1,), (1,)), ((), ())), preferred_element_type=f32)
    scores = precision[None, :] * (correlation - half_norm[:, None])
    distance = jnp.abs(rotation_ids[:, None] - prev_rotation[None, :])
    distance = jnp.minimum(distance, R - distance).astype(f32)
    width = R / 8.0
    match = (class_ids[:, None] == prev_class[None, :]).astype(f32)
    scores = scores + (-distance * distance / (2.0 * width * width) + match)
    local_top = jnp.max(scores, axis=0)
    local_mass = jnp.sum(jnp.exp(scores - local_top[None, :]), axis=0)
    stats = jnp.stack([local_top, local_mass])
    stats = exchange(jnp.broadcast_to(stats, (8, 2, P_DEV)), CLS)
    top_score = jnp.max(stats[:, 0], axis=0)
    total_mass = jnp.sum(stats[:, 1] * jnp.exp(stats[:, 0] - top_score[None, :]), axis=0)
    probs = jnp.exp(scores - top_score[None, :]) / total_mass[None, :]
    weights = probs.astype(bf16)
    numerator = lax.dot_general(weights, shifted, (((1,), (0,)), ((), ())), preferred_element_type=f32)
    summed, mass = scatter_sums(numerator, jnp.sum(probs, axis=1))
    refreshed = summed / (mass[:, :, None, None] + 1.0)
    evidence = top_score + jnp.log(total_mass)
    return (refreshed.reshape(K, TILES * 128), evidence)


def solution(mesh):
    split = Mesh(mesh.devices.reshape(4, 2, 4, 2, 2, 4), DOM + CLS)
    return jax.shard_map(
        on_device,
        mesh=split,
        in_specs=(P(DOM, None), P(DOM), P(DOM), P(DOM), P(DOM), P(CLS, DOM)),
        out_specs=(P(CLS, DOM), P(DOM)),
        check_vma=False,
    )
```

```python
import math

import jax
import jax.numpy as jnp
from jax import lax
from jax.experimental import pallas as pl
from jax.experimental.pallas import tpu as pltpu
from jax.sharding import Mesh
from jax.sharding import PartitionSpec as P

BOX = 64
F = 4096
H = F // 2
R = 24
K = 8
ROWS = K * R
SHIFTS = 25
SIDE = 5
P_DEV = 576
ROW_BLOCK = 96
TILES = 12

bf16 = jnp.bfloat16
f32 = jnp.float32

Z = ("za", "zb")
CLS = ("zh", "x")
DOM = ("y", "za", "zb", "c")


def phase_table():
    frequency = jnp.arange(H, dtype=jnp.int32)
    freq_x = frequency % BOX - BOX // 2
    freq_y = frequency // BOX
    shift = jnp.arange(SHIFTS, dtype=jnp.int32)
    step_x = shift % SIDE - 2
    step_y = shift // SIDE - 2
    phase = (freq_x[None, :] * step_x[:, None] + freq_y[None, :] * step_y[:, None]) % BOX
    angle = phase.astype(f32) * (2.0 * math.pi / BOX)
    exact = jnp.concatenate([jnp.cos(angle), jnp.sin(angle)], axis=1)
    high = lax.reduce_precision(exact, 8, 7)
    rest = exact - high
    middle = lax.reduce_precision(rest, 8, 7)
    low = rest - middle
    return jnp.concatenate([high, middle, low, jnp.zeros((128 - 3 * SHIFTS, F), f32)], axis=0).astype(bf16)


def shift_kernel(index_ref, table_ref, image_ref, out_ref):
    index = index_ref[...]
    lane = lax.broadcasted_iota(jnp.int32, (ROW_BLOCK, 128), 1)
    chosen = (lane == index) | (lane == index + SHIFTS) | (lane == index + 2 * SHIFTS)
    chosen = jnp.where(chosen, 1.0, 0.0).astype(bf16)
    for at in range(0, H, 512):
        cosine = jnp.dot(chosen, table_ref[:, at : at + 512], preferred_element_type=f32)
        sine = jnp.dot(chosen, table_ref[:, H + at : H + at + 512], preferred_element_type=f32)
        real = image_ref[:, at : at + 512].astype(f32)
        imag = image_ref[:, H + at : H + at + 512].astype(f32)
        out_ref[:, at : at + 512] = (real * cosine + imag * sine).astype(bf16)
        out_ref[:, H + at : H + at + 512] = (imag * cosine - real * sine).astype(bf16)


def shift_particles(particles, shift_index):
    return pl.pallas_call(
        shift_kernel,
        grid=(P_DEV // ROW_BLOCK,),
        in_specs=[
            pl.BlockSpec((ROW_BLOCK, 1), lambda i: (i, 0)),
            pl.BlockSpec((128, F), lambda i: (0, 0)),
            pl.BlockSpec((ROW_BLOCK, F), lambda i: (i, 0)),
        ],
        out_specs=pl.BlockSpec((ROW_BLOCK, F), lambda i: (i, 0)),
        out_shape=pltpu.HBM((P_DEV, F), bf16),
        compiler_params=pltpu.CompilerParams(vmem_limit_bytes=16 << 20),
        name="shift",
    )(shift_index[:, None], phase_table(), particles)


def exchange(array, axis):
    return lax.all_to_all(array, axis, 0, 0, tiled=True)


def gather_table(references, shifted_of):
    mine = references.reshape(K, TILES, 128).transpose(1, 0, 2)
    along_z = exchange(jnp.broadcast_to(mine, (8, TILES, K, 128)), Z)
    along_z, shifted = lax.optimization_barrier((along_z, shifted_of()))
    along_y = exchange(jnp.broadcast_to(along_z, (4, 8, TILES, K, 128)), "y")
    other = lax.ppermute(along_y, "c", [(0, 1), (1, 0)])
    return along_y.reshape(8, 4, TILES, K, 128), other.reshape(8, 4, TILES, K, 128), shifted


def column_copies(source_ref, target_ref, arrived):
    copies = []
    for q in range(8):
        columns = pl.ds(q * 512, 512)
        copies.append(pltpu.make_async_copy(source_ref.at[:, columns], target_ref.at[:, columns], arrived.at[q]))
        copies[-1].start()
    return copies


def score_kernel(place_ref, own_ref, other_ref, shifted_ref, class_ref, rotation_ref, precision_ref, scores_ref, stats_ref, table_ref, images_ref, arrived):
    copies = column_copies(shifted_ref, images_ref, arrived)
    core = place_ref[0]
    for source, at in ((own_ref, core), (other_ref, 1 - core)):
        for zb in range(4):
            for b in range(3):
                part = 6 * zb + 3 * at + b
                turn = part // 8
                column = (part - 8 * turn) * 512
                rows = pl.ds(pl.multiple_of(turn * 64, 64), 64)
                for lanes in range(4):
                    tiles = source[:, zb, 4 * b + lanes].reshape(64, 128)
                    table_ref[rows, pl.ds(pl.multiple_of(column + lanes * 128, 128), 128)] = tiles
    half_norm = jnp.zeros((ROWS, 128), f32)
    for at in range(0, F, 128):
        piece = table_ref[:, at : at + 128].astype(f32)
        half_norm = half_norm + piece * piece
    half_norm = 0.5 * jnp.sum(half_norm, axis=1, keepdims=True)
    for copy in copies:
        copy.wait()
    correlation = lax.dot_general(table_ref[...], images_ref[...], (((1,), (1,)), ((), ())), preferred_element_type=f32)
    row = lax.broadcasted_iota(jnp.int32, (ROWS, 1), 0)
    class_ids = place_ref[1] + row % K
    rotation_ids = (row // K) % 8 * 3 + row // 64
    distance = jnp.abs(rotation_ids - rotation_ref[...])
    distance = jnp.minimum(distance, R - distance).astype(f32)
    width = R / 8.0
    match = jnp.where(class_ids == class_ref[...], 1.0, 0.0)
    scores = precision_ref[...] * (correlation - half_norm) + (-distance * distance / (2.0 * width * width) + match)
    scores_ref[...] = scores
    top = jnp.max(scores, axis=0, keepdims=True)
    mass = jnp.sum(jnp.exp(scores - top), axis=0, keepdims=True)
    for at in range(8):
        stats_ref[at, 0:1, :] = top
        stats_ref[at, 1:2, :] = mass


def local_scores(own, other, shifted, prev_class, prev_rotation, precision):
    place = jnp.stack([lax.axis_index("c"), lax.axis_index(CLS) * K]).astype(jnp.int32)
    vmem = pl.BlockSpec(memory_space=pltpu.VMEM)
    return pl.pallas_call(
        score_kernel,
        in_specs=[pl.BlockSpec(memory_space=pltpu.SMEM), vmem, vmem, pl.BlockSpec(memory_space=pltpu.HBM)] + [vmem] * 3,
        out_specs=[vmem, vmem],
        out_shape=[jax.ShapeDtypeStruct((ROWS, P_DEV), f32), jax.ShapeDtypeStruct((8, 2, P_DEV), f32)],
        scratch_shapes=[pltpu.VMEM((ROWS, F), bf16), pltpu.VMEM((P_DEV, F), bf16), pltpu.SemaphoreType.DMA((8,))],
        compiler_params=pltpu.CompilerParams(vmem_limit_bytes=16 << 20),
        name="scores",
    )(place, own, other, shifted, prev_class[None, :], prev_rotation[None, :], precision[None, :])


def sum_kernel(stats_ref, scores_ref, shifted_ref, pieces_ref, evidence_ref, images_ref, arrived):
    copies = column_copies(shifted_ref, images_ref, arrived)
    tops = [stats_ref[i, 0:1, :] for i in range(8)]
    top = tops[0]
    for i in range(1, 8):
        top = jnp.maximum(top, tops[i])
    mass = jnp.zeros_like(top)
    for i in range(8):
        mass = mass + stats_ref[i, 1:2, :] * jnp.exp(tops[i] - top)
    evidence_ref[...] = top + jnp.log(mass)
    probs = jnp.exp(scores_ref[...] - top) * (1.0 / mass)
    weights = probs.astype(bf16)
    occupancy = jnp.sum(probs, axis=1, keepdims=True)
    high = occupancy.astype(bf16).astype(f32)
    low = occupancy - high
    lane = lax.broadcasted_iota(jnp.int32, (8, K, 128), 2)
    high = [high[64 * turn : 64 * turn + 64].reshape(8, K, 1) for turn in range(3)]
    low = [low[64 * turn : 64 * turn + 64].reshape(8, K, 1) for turn in range(3)]
    for j in range(8):
        tile = jnp.zeros((8, K, 128), f32)
        for b in range(3):
            turn = (3 * j + b) // 8
            tile = jnp.where(lane == b, high[turn], tile)
            tile = jnp.where(lane == 3 + b, low[turn], tile)
        pieces_ref[j % 2, :, j // 2, TILES] = tile.astype(bf16)
    for q in range(8):
        copies[q].wait()
        numerator = jnp.dot(weights, images_ref[:, q * 512 : q * 512 + 512], preferred_element_type=f32)
        for turn in range(3):
            part = 8 * turn + q
            j, b = part // 3, part % 3
            for lanes in range(4):
                tile = numerator[64 * turn : 64 * turn + 64, 128 * lanes : 128 * lanes + 128]
                pieces_ref[j % 2, :, j // 2, 4 * b + lanes] = tile.reshape(8, K, 128).astype(bf16)


def local_sums(stats, scores, shifted):
    vmem = pl.BlockSpec(memory_space=pltpu.VMEM)
    return pl.pallas_call(
        sum_kernel,
        in_specs=[vmem, vmem, pl.BlockSpec(memory_space=pltpu.HBM)],
        out_specs=[vmem, vmem],
        out_shape=[
            jax.ShapeDtypeStruct((2, 8, 4, TILES + 1, K, 128), bf16),
            jax.ShapeDtypeStruct((1, P_DEV), f32),
        ],
        scratch_shapes=[pltpu.VMEM((P_DEV, F), bf16), pltpu.SemaphoreType.DMA((8,))],
        compiler_params=pltpu.CompilerParams(vmem_limit_bytes=16 << 20),
        name="sums",
    )(stats, scores, shifted)


def scatter_sums(pieces):
    pieces = exchange(pieces, "c").astype(f32)
    pieces = jnp.sum(pieces, axis=0).astype(bf16)
    pieces = pieces.reshape(4, 8, TILES + 1, K, 128)
    pieces = exchange(pieces, "y").astype(f32)
    pieces = jnp.sum(pieces, axis=0).astype(bf16)
    pieces = exchange(pieces, Z).astype(f32)
    pieces = jnp.sum(pieces, axis=0)
    summed = pieces[:TILES].reshape(3, 4, K, 128).transpose(2, 0, 1, 3)
    mass = pieces[TILES, :, 0:3] + pieces[TILES, :, 3:6]
    return summed, mass


def on_device(particles, shift_index, prev_class, prev_rotation, precision, references):
    own, other, shifted = gather_table(references, lambda: shift_particles(particles, shift_index))
    shifted = pltpu.with_memory_space_constraint(shifted, pltpu.HBM)
    scores, stats = local_scores(own, other, shifted, prev_class, prev_rotation, precision)
    stats = exchange(stats, CLS)
    pieces, evidence = local_sums(stats, scores, shifted)
    summed, mass = scatter_sums(pieces)
    refreshed = summed / (mass[:, :, None, None] + 1.0)
    return (refreshed.reshape(K, TILES * 128), evidence.reshape(P_DEV))


def solution(mesh):
    split = Mesh(mesh.devices.reshape(4, 2, 4, 2, 2, 4), DOM + CLS)
    return jax.shard_map(
        on_device,
        mesh=split,
        in_specs=(P(DOM, None), P(DOM), P(DOM), P(DOM), P(DOM), P(CLS, DOM)),
        out_specs=(P(CLS, DOM), P(DOM)),
        check_vma=False,
    )
```

```python
import math

import jax
import jax.numpy as jnp
from jax import lax
from jax.experimental import pallas as pl
from jax.experimental.pallas import tpu as pltpu
from jax.sharding import Mesh
from jax.sharding import PartitionSpec as P

BOX = 64
F = 4096
H = F // 2
R = 24
K = 8
ROWS = K * R
SHIFTS = 25
SIDE = 5
P_DEV = 576
ROW_BLOCK = 96
TILES = 12

bf16 = jnp.bfloat16
f32 = jnp.float32

Z = ("za", "zb")
CLS = ("zh", "x")
DOM = ("y", "za", "zb", "c")


def phase_table():
    frequency = jnp.arange(H, dtype=jnp.int32)
    freq_x = frequency % BOX - BOX // 2
    freq_y = frequency // BOX
    shift = jnp.arange(SHIFTS, dtype=jnp.int32)
    step_x = shift % SIDE - 2
    step_y = shift // SIDE - 2
    phase = (freq_x[None, :] * step_x[:, None] + freq_y[None, :] * step_y[:, None]) % BOX
    angle = phase.astype(f32) * (2.0 * math.pi / BOX)
    exact = jnp.concatenate([jnp.cos(angle), jnp.sin(angle)], axis=1)
    high = lax.reduce_precision(exact, 8, 7)
    rest = exact - high
    middle = lax.reduce_precision(rest, 8, 7)
    low = rest - middle
    return jnp.concatenate([high, middle, low, jnp.zeros((128 - 3 * SHIFTS, F), f32)], axis=0).astype(bf16)


def shift_kernel(index_ref, table_ref, image_ref, out_ref):
    index = index_ref[...]
    lane = lax.broadcasted_iota(jnp.int32, (ROW_BLOCK, 128), 1)
    chosen = (lane == index) | (lane == index + SHIFTS) | (lane == index + 2 * SHIFTS)
    chosen = jnp.where(chosen, 1.0, 0.0).astype(bf16)
    for at in range(0, H, 512):
        cosine = jnp.dot(chosen, table_ref[:, at : at + 512], preferred_element_type=f32)
        sine = jnp.dot(chosen, table_ref[:, H + at : H + at + 512], preferred_element_type=f32)
        real = image_ref[:, at : at + 512].astype(f32)
        imag = image_ref[:, H + at : H + at + 512].astype(f32)
        out_ref[:, at : at + 512] = (real * cosine + imag * sine).astype(bf16)
        out_ref[:, H + at : H + at + 512] = (imag * cosine - real * sine).astype(bf16)


def shift_particles(particles, shift_index, table):
    return pl.pallas_call(
        shift_kernel,
        grid=(P_DEV // ROW_BLOCK,),
        in_specs=[
            pl.BlockSpec((ROW_BLOCK, 1), lambda i: (i, 0)),
            pl.BlockSpec((128, F), lambda i: (0, 0)),
            pl.BlockSpec((ROW_BLOCK, F), lambda i: (i, 0)),
        ],
        out_specs=pl.BlockSpec((ROW_BLOCK, F), lambda i: (i, 0)),
        out_shape=pltpu.HBM((P_DEV, F), bf16),
        compiler_params=pltpu.CompilerParams(vmem_limit_bytes=16 << 20),
        name="shift",
    )(shift_index, table, particles)


def exchange(array, axis):
    return lax.all_to_all(array, axis, 0, 0, tiled=True)


def gather_table(references, particles, shift_index):
    mine = references.reshape(K, TILES, 128).transpose(1, 0, 2)
    along_z = exchange(jnp.broadcast_to(mine, (8, TILES, K, 128)), Z)
    along_z, index, phases = lax.optimization_barrier((along_z, shift_index[:, None], phase_table()))
    along_y = exchange(jnp.broadcast_to(along_z, (4, 8, TILES, K, 128)), "y")
    along_y, shifted = lax.optimization_barrier((along_y, shift_particles(particles, index, phases)))
    other = lax.ppermute(along_y, "c", [(0, 1), (1, 0)])
    return along_y.reshape(8, 4, TILES, K, 128), other.reshape(8, 4, TILES, K, 128), shifted


def column_copies(source_ref, target_ref, arrived):
    copies = []
    for q in range(8):
        columns = pl.ds(q * 512, 512)
        copies.append(pltpu.make_async_copy(source_ref.at[:, columns], target_ref.at[:, columns], arrived.at[q]))
        copies[-1].start()
    return copies


def score_kernel(place_ref, own_ref, other_ref, shifted_ref, class_ref, rotation_ref, precision_ref, scores_ref, stats_ref, table_ref, images_ref, arrived):
    copies = column_copies(shifted_ref, images_ref, arrived)
    core = place_ref[0]
    for source, at in ((own_ref, core), (other_ref, 1 - core)):
        for zb in range(4):
            for b in range(3):
                part = 6 * zb + 3 * at + b
                turn = part // 8
                column = (part - 8 * turn) * 512
                rows = pl.ds(pl.multiple_of(turn * 64, 64), 64)
                for lanes in range(4):
                    tiles = source[:, zb, 4 * b + lanes].reshape(64, 128)
                    table_ref[rows, pl.ds(pl.multiple_of(column + lanes * 128, 128), 128)] = tiles
    half_norm = jnp.zeros((ROWS, 128), f32)
    for at in range(0, F, 128):
        piece = table_ref[:, at : at + 128].astype(f32)
        half_norm = half_norm + piece * piece
    half_norm = 0.5 * jnp.sum(half_norm, axis=1, keepdims=True)
    for copy in copies:
        copy.wait()
    correlation = lax.dot_general(table_ref[...], images_ref[...], (((1,), (1,)), ((), ())), preferred_element_type=f32)
    row = lax.broadcasted_iota(jnp.int32, (ROWS, 1), 0)
    class_ids = place_ref[1] + row % K
    rotation_ids = (row // K) % 8 * 3 + row // 64
    distance = jnp.abs(rotation_ids - rotation_ref[...])
    distance = jnp.minimum(distance, R - distance).astype(f32)
    width = R / 8.0
    match = jnp.where(class_ids == class_ref[...], 1.0, 0.0)
    scores = precision_ref[...] * (correlation - half_norm) + (-distance * distance / (2.0 * width * width) + match)
    scores_ref[...] = scores
    top = jnp.max(scores, axis=0, keepdims=True)
    mass = jnp.sum(jnp.exp(scores - top), axis=0, keepdims=True)
    for at in range(8):
        stats_ref[at, 0:1, :] = top
        stats_ref[at, 1:2, :] = mass


def local_scores(own, other, shifted, prev_class, prev_rotation, precision):
    place = jnp.stack([lax.axis_index("c"), lax.axis_index(CLS) * K]).astype(jnp.int32)
    vmem = pl.BlockSpec(memory_space=pltpu.VMEM)
    return pl.pallas_call(
        score_kernel,
        in_specs=[pl.BlockSpec(memory_space=pltpu.SMEM), vmem, vmem, pl.BlockSpec(memory_space=pltpu.HBM)] + [vmem] * 3,
        out_specs=[vmem, vmem],
        out_shape=[jax.ShapeDtypeStruct((ROWS, P_DEV), f32), jax.ShapeDtypeStruct((8, 2, P_DEV), f32)],
        scratch_shapes=[pltpu.VMEM((ROWS, F), bf16), pltpu.VMEM((P_DEV, F), bf16), pltpu.SemaphoreType.DMA((8,))],
        compiler_params=pltpu.CompilerParams(vmem_limit_bytes=16 << 20),
        name="scores",
    )(place, own, other, shifted, prev_class[None, :], prev_rotation[None, :], precision[None, :])


def sum_kernel(stats_ref, scores_ref, shifted_ref, pieces_ref, evidence_ref, images_ref, arrived):
    copies = column_copies(shifted_ref, images_ref, arrived)
    tops = [stats_ref[i, 0:1, :] for i in range(8)]
    top = tops[0]
    for i in range(1, 8):
        top = jnp.maximum(top, tops[i])
    mass = jnp.zeros_like(top)
    for i in range(8):
        mass = mass + stats_ref[i, 1:2, :] * jnp.exp(tops[i] - top)
    evidence_ref[...] = top + jnp.log(mass)
    probs = jnp.exp(scores_ref[...] - top) * (1.0 / mass)
    weights = probs.astype(bf16)
    occupancy = jnp.sum(probs, axis=1, keepdims=True)
    high = occupancy.astype(bf16).astype(f32)
    low = occupancy - high
    lane = lax.broadcasted_iota(jnp.int32, (8, K, 128), 2)
    high = [high[64 * turn : 64 * turn + 64].reshape(8, K, 1) for turn in range(3)]
    low = [low[64 * turn : 64 * turn + 64].reshape(8, K, 1) for turn in range(3)]
    for j in range(8):
        tile = jnp.zeros((8, K, 128), f32)
        for b in range(3):
            turn = (3 * j + b) // 8
            tile = jnp.where(lane == b, high[turn], tile)
            tile = jnp.where(lane == 3 + b, low[turn], tile)
        pieces_ref[j % 2, :, j // 2, TILES] = tile.astype(bf16)
    for q in range(8):
        copies[q].wait()
        numerator = jnp.dot(weights, images_ref[:, q * 512 : q * 512 + 512], preferred_element_type=f32)
        for turn in range(3):
            part = 8 * turn + q
            j, b = part // 3, part % 3
            for lanes in range(4):
                tile = numerator[64 * turn : 64 * turn + 64, 128 * lanes : 128 * lanes + 128]
                pieces_ref[j % 2, :, j // 2, 4 * b + lanes] = tile.reshape(8, K, 128).astype(bf16)


def local_sums(stats, scores, shifted):
    vmem = pl.BlockSpec(memory_space=pltpu.VMEM)
    return pl.pallas_call(
        sum_kernel,
        in_specs=[vmem, vmem, pl.BlockSpec(memory_space=pltpu.HBM)],
        out_specs=[vmem, vmem],
        out_shape=[
            jax.ShapeDtypeStruct((2, 8, 4, TILES + 1, K, 128), bf16),
            jax.ShapeDtypeStruct((1, P_DEV), f32),
        ],
        scratch_shapes=[pltpu.VMEM((P_DEV, F), bf16), pltpu.SemaphoreType.DMA((8,))],
        compiler_params=pltpu.CompilerParams(vmem_limit_bytes=16 << 20),
        name="sums",
    )(stats, scores, shifted)


def finish_kernel(pieces_ref, out_ref):
    total = pieces_ref[0].astype(f32)
    for i in range(1, 8):
        total = total + pieces_ref[i].astype(f32)
    mass = total[TILES]
    for b in range(3):
        scale = 1.0 / (mass[:, b : b + 1] + mass[:, 3 + b : 4 + b] + 1.0)
        for lanes in range(4):
            at = 4 * b + lanes
            out_ref[:, at * 128 : at * 128 + 128] = total[at] * scale


def scatter_sums(pieces):
    pieces = exchange(pieces, "c").astype(f32)
    pieces = jnp.sum(pieces, axis=0).astype(bf16)
    pieces = pieces.reshape(4, 8, TILES + 1, K, 128)
    pieces = exchange(pieces, "y").astype(f32)
    pieces = jnp.sum(pieces, axis=0).astype(bf16)
    pieces = exchange(pieces, Z)
    return pl.pallas_call(
        finish_kernel,
        out_shape=jax.ShapeDtypeStruct((K, TILES * 128), f32),
        compiler_params=pltpu.CompilerParams(vmem_limit_bytes=16 << 20),
        name="finish",
    )(pieces.reshape(8, TILES + 1, K, 128))


def on_device(particles, shift_index, prev_class, prev_rotation, precision, references):
    own, other, shifted = gather_table(references, particles, shift_index)
    shifted = pltpu.with_memory_space_constraint(shifted, pltpu.HBM)
    scores, stats = local_scores(own, other, shifted, prev_class, prev_rotation, precision)
    stats = exchange(stats, CLS)
    pieces, evidence = local_sums(stats, scores, shifted)
    return (scatter_sums(pieces), evidence.reshape(P_DEV))


def solution(mesh):
    split = Mesh(mesh.devices.reshape(4, 2, 4, 2, 2, 4), DOM + CLS)
    return jax.shard_map(
        on_device,
        mesh=split,
        in_specs=(P(DOM, None), P(DOM), P(DOM), P(DOM), P(DOM), P(CLS, DOM)),
        out_specs=(P(CLS, DOM), P(DOM)),
        check_vma=False,
    )
```

```python
import math

import jax
import jax.numpy as jnp
from jax import lax
from jax.experimental import pallas as pl
from jax.experimental.pallas import tpu as pltpu
from jax.sharding import Mesh
from jax.sharding import PartitionSpec as P

BOX = 64
F = 4096
H = F // 2
R = 24
K = 8
ROWS = K * R
SHIFTS = 25
SIDE = 5
P_DEV = 576
ROW_BLOCK = 96
TILES = 12

bf16 = jnp.bfloat16
f32 = jnp.float32

Z = ("za", "zb")
CLS = ("zh", "x")
DOM = ("y", "za", "zb", "c")


def phase_table():
    frequency = jnp.arange(H, dtype=jnp.int32)
    freq_x = frequency % BOX - BOX // 2
    freq_y = frequency // BOX
    shift = jnp.arange(SHIFTS, dtype=jnp.int32)
    step_x = shift % SIDE - 2
    step_y = shift // SIDE - 2
    phase = (freq_x[None, :] * step_x[:, None] + freq_y[None, :] * step_y[:, None]) % BOX
    angle = phase.astype(f32) * (2.0 * math.pi / BOX)
    exact = jnp.concatenate([jnp.cos(angle), jnp.sin(angle)], axis=1)
    high = lax.reduce_precision(exact, 8, 7)
    rest = exact - high
    middle = lax.reduce_precision(rest, 8, 7)
    low = rest - middle
    return jnp.concatenate([high, middle, low, jnp.zeros((128 - 3 * SHIFTS, F), f32)], axis=0).astype(bf16)


def shift_kernel(index_ref, table_ref, image_ref, out_ref):
    index = index_ref[...]
    lane = lax.broadcasted_iota(jnp.int32, (ROW_BLOCK, 128), 1)
    chosen = (lane == index) | (lane == index + SHIFTS) | (lane == index + 2 * SHIFTS)
    chosen = jnp.where(chosen, 1.0, 0.0).astype(bf16)
    for at in range(0, H, 512):
        cosine = jnp.dot(chosen, table_ref[:, at : at + 512], preferred_element_type=f32)
        sine = jnp.dot(chosen, table_ref[:, H + at : H + at + 512], preferred_element_type=f32)
        real = image_ref[:, at : at + 512].astype(f32)
        imag = image_ref[:, H + at : H + at + 512].astype(f32)
        out_ref[:, at : at + 512] = (real * cosine + imag * sine).astype(bf16)
        out_ref[:, H + at : H + at + 512] = (imag * cosine - real * sine).astype(bf16)


def shift_particles(particles, shift_index, table):
    return pl.pallas_call(
        shift_kernel,
        grid=(P_DEV // ROW_BLOCK,),
        in_specs=[
            pl.BlockSpec((ROW_BLOCK, 1), lambda i: (i, 0)),
            pl.BlockSpec((128, F), lambda i: (0, 0)),
            pl.BlockSpec((ROW_BLOCK, F), lambda i: (i, 0)),
        ],
        out_specs=pl.BlockSpec((ROW_BLOCK, F), lambda i: (i, 0)),
        out_shape=pltpu.HBM((P_DEV, F), bf16),
        compiler_params=pltpu.CompilerParams(vmem_limit_bytes=16 << 20),
        name="shift",
    )(shift_index, table, particles)


def exchange(array, axis):
    return lax.all_to_all(array, axis, 0, 0, tiled=True)


def gather_table(references, particles, shift_index):
    mine = references.reshape(K, TILES, 128).transpose(1, 0, 2)
    along_z = exchange(jnp.broadcast_to(mine, (8, TILES, K, 128)), Z)
    along_z, index, phases = lax.optimization_barrier((along_z, shift_index[:, None], phase_table()))
    along_y = exchange(jnp.broadcast_to(along_z, (4, 8, TILES, K, 128)), "y")
    along_y, shifted = lax.optimization_barrier((along_y, shift_particles(particles, index, phases)))
    other = lax.ppermute(along_y, "c", [(0, 1), (1, 0)])
    return along_y.reshape(8, 4, TILES, K, 128), other.reshape(8, 4, TILES, K, 128), shifted


def fill_table(source_ref, table_ref, core):
    for zb in range(4):
        for b in range(3):
            part = 6 * zb + 3 * core + b
            turn = part // 8
            column = (part - 8 * turn) * 512
            rows = pl.ds(pl.multiple_of(turn * 64, 64), 64)
            for lanes in range(4):
                tiles = source_ref[:, zb, 4 * b + lanes].reshape(64, 128)
                table_ref[rows, pl.ds(pl.multiple_of(column + lanes * 128, 128), 128)] = tiles


def load_kernel(place_ref, own_ref, shifted_ref, images_ref, table_ref, arrived):
    copies = []
    for q in range(8):
        columns = pl.ds(q * 512, 512)
        copies.append(pltpu.make_async_copy(shifted_ref.at[:, columns], images_ref.at[:, columns], arrived.at[q]))
        copies[-1].start()
    fill_table(own_ref, table_ref, place_ref[0])
    for copy in copies:
        copy.wait()


def load_own(place, own, shifted):
    vmem = pl.BlockSpec(memory_space=pltpu.VMEM)
    return pl.pallas_call(
        load_kernel,
        in_specs=[pl.BlockSpec(memory_space=pltpu.SMEM), vmem, pl.BlockSpec(memory_space=pltpu.HBM)],
        out_specs=[vmem, vmem],
        out_shape=[pltpu.VMEM((P_DEV, F), bf16), pltpu.VMEM((ROWS, F), bf16)],
        scratch_shapes=[pltpu.SemaphoreType.DMA((8,))],
        compiler_params=pltpu.CompilerParams(vmem_limit_bytes=16 << 20),
        name="load",
    )(place, own, pltpu.with_memory_space_constraint(shifted, pltpu.HBM))


def score_kernel(place_ref, other_ref, half_ref, shifted_ref, class_ref, rotation_ref, precision_ref, scores_ref, stats_ref, table_ref):
    fill_table(other_ref, table_ref, 1 - place_ref[0])
    half_norm = jnp.zeros((ROWS, 128), f32)
    for at in range(0, F, 128):
        piece = table_ref[:, at : at + 128].astype(f32)
        half_norm = half_norm + piece * piece
    half_norm = 0.5 * jnp.sum(half_norm, axis=1, keepdims=True)
    correlation = lax.dot_general(table_ref[...], shifted_ref[...], (((1,), (1,)), ((), ())), preferred_element_type=f32)
    row = lax.broadcasted_iota(jnp.int32, (ROWS, 1), 0)
    class_ids = place_ref[1] + row % K
    rotation_ids = (row // K) % 8 * 3 + row // 64
    distance = jnp.abs(rotation_ids - rotation_ref[...])
    distance = jnp.minimum(distance, R - distance).astype(f32)
    width = R / 8.0
    match = jnp.where(class_ids == class_ref[...], 1.0, 0.0)
    scores = precision_ref[...] * (correlation - half_norm) + (-distance * distance / (2.0 * width * width) + match)
    scores_ref[...] = scores
    top = jnp.max(scores, axis=0, keepdims=True)
    mass = jnp.sum(jnp.exp(scores - top), axis=0, keepdims=True)
    for at in range(8):
        stats_ref[at, 0:1, :] = top
        stats_ref[at, 1:2, :] = mass


def local_scores(own, other, shifted, prev_class, prev_rotation, precision):
    place = jnp.stack([lax.axis_index("c"), lax.axis_index(CLS) * K]).astype(jnp.int32)
    images, half = load_own(place, own, shifted)
    vmem = pl.BlockSpec(memory_space=pltpu.VMEM)
    scores, stats, _ = pl.pallas_call(
        score_kernel,
        in_specs=[pl.BlockSpec(memory_space=pltpu.SMEM)] + [vmem] * 6,
        out_specs=[vmem, vmem, vmem],
        out_shape=[jax.ShapeDtypeStruct((ROWS, P_DEV), f32), jax.ShapeDtypeStruct((8, 2, P_DEV), f32), pltpu.VMEM((ROWS, F), bf16)],
        input_output_aliases={2: 2},
        compiler_params=pltpu.CompilerParams(vmem_limit_bytes=16 << 20),
        name="scores",
    )(place, other, half, images, prev_class[None, :], prev_rotation[None, :], precision[None, :])
    return scores, stats, images


def sum_kernel(stats_ref, scores_ref, shifted_ref, pieces_ref, evidence_ref):
    tops = [stats_ref[i, 0:1, :] for i in range(8)]
    top = tops[0]
    for i in range(1, 8):
        top = jnp.maximum(top, tops[i])
    mass = jnp.zeros_like(top)
    for i in range(8):
        mass = mass + stats_ref[i, 1:2, :] * jnp.exp(tops[i] - top)
    evidence_ref[...] = top + jnp.log(mass)
    probs = jnp.exp(scores_ref[...] - top) * (1.0 / mass)
    weights = probs.astype(bf16)
    occupancy = jnp.sum(probs, axis=1, keepdims=True)
    high = occupancy.astype(bf16).astype(f32)
    low = occupancy - high
    lane = lax.broadcasted_iota(jnp.int32, (8, K, 128), 2)
    high = [high[64 * turn : 64 * turn + 64].reshape(8, K, 1) for turn in range(3)]
    low = [low[64 * turn : 64 * turn + 64].reshape(8, K, 1) for turn in range(3)]
    for j in range(8):
        tile = jnp.zeros((8, K, 128), f32)
        for b in range(3):
            turn = (3 * j + b) // 8
            tile = jnp.where(lane == b, high[turn], tile)
            tile = jnp.where(lane == 3 + b, low[turn], tile)
        pieces_ref[j % 2, :, j // 2, TILES] = tile.astype(bf16)
    for q in range(8):
        numerator = jnp.dot(weights, shifted_ref[:, q * 512 : q * 512 + 512], preferred_element_type=f32)
        for turn in range(3):
            part = 8 * turn + q
            j, b = part // 3, part % 3
            for lanes in range(4):
                tile = numerator[64 * turn : 64 * turn + 64, 128 * lanes : 128 * lanes + 128]
                pieces_ref[j % 2, :, j // 2, 4 * b + lanes] = tile.reshape(8, K, 128).astype(bf16)


def local_sums(stats, scores, shifted):
    vmem = pl.BlockSpec(memory_space=pltpu.VMEM)
    return pl.pallas_call(
        sum_kernel,
        in_specs=[vmem, vmem, vmem],
        out_specs=[vmem, vmem],
        out_shape=[
            jax.ShapeDtypeStruct((2, 8, 4, TILES + 1, K, 128), bf16),
            jax.ShapeDtypeStruct((1, P_DEV), f32),
        ],
        compiler_params=pltpu.CompilerParams(vmem_limit_bytes=16 << 20),
        name="sums",
    )(stats, scores, shifted)


def finish_kernel(pieces_ref, out_ref):
    total = pieces_ref[0].astype(f32)
    for i in range(1, 8):
        total = total + pieces_ref[i].astype(f32)
    mass = total[TILES]
    for b in range(3):
        scale = 1.0 / (mass[:, b : b + 1] + mass[:, 3 + b : 4 + b] + 1.0)
        for lanes in range(4):
            at = 4 * b + lanes
            out_ref[:, at * 128 : at * 128 + 128] = total[at] * scale


def scatter_sums(pieces):
    pieces = exchange(pieces, "c").astype(f32)
    pieces = jnp.sum(pieces, axis=0).astype(bf16)
    pieces = pieces.reshape(4, 8, TILES + 1, K, 128)
    pieces = exchange(pieces, "y").astype(f32)
    pieces = jnp.sum(pieces, axis=0).astype(bf16)
    pieces = exchange(pieces, Z)
    return pl.pallas_call(
        finish_kernel,
        out_shape=jax.ShapeDtypeStruct((K, TILES * 128), f32),
        compiler_params=pltpu.CompilerParams(vmem_limit_bytes=16 << 20),
        name="finish",
    )(pieces.reshape(8, TILES + 1, K, 128))


def on_device(particles, shift_index, prev_class, prev_rotation, precision, references):
    own, other, shifted = gather_table(references, particles, shift_index)
    scores, stats, images = local_scores(own, other, shifted, prev_class, prev_rotation, precision)
    stats = exchange(stats, CLS)
    pieces, evidence = local_sums(stats, scores, images)
    return (scatter_sums(pieces), evidence.reshape(P_DEV))


def solution(mesh):
    split = Mesh(mesh.devices.reshape(4, 2, 4, 2, 2, 4), DOM + CLS)
    return jax.shard_map(
        on_device,
        mesh=split,
        in_specs=(P(DOM, None), P(DOM), P(DOM), P(DOM), P(DOM), P(CLS, DOM)),
        out_specs=(P(CLS, DOM), P(DOM)),
        check_vma=False,
    )
```

```python
import math

import jax
import jax.numpy as jnp
from jax import lax
from jax.experimental import pallas as pl
from jax.experimental.pallas import tpu as pltpu
from jax.sharding import Mesh
from jax.sharding import PartitionSpec as P

BOX = 64
F = 4096
H = F // 2
R = 24
K = 8
ROWS = K * R
SHIFTS = 25
SIDE = 5
P_DEV = 576
ROW_BLOCK = 96
TILES = 12
PIECES = 96

bf16 = jnp.bfloat16
f32 = jnp.float32

Z = ("za", "zb")
CLS = ("zh", "x")
DOM = ("y", "za", "zb", "c")


def phase_table():
    frequency = jnp.arange(H, dtype=jnp.int32)
    freq_x = frequency % BOX - BOX // 2
    freq_y = frequency // BOX
    shift = jnp.arange(SHIFTS, dtype=jnp.int32)
    step_x = shift % SIDE - 2
    step_y = shift // SIDE - 2
    phase = (freq_x[None, :] * step_x[:, None] + freq_y[None, :] * step_y[:, None]) % BOX
    angle = phase.astype(f32) * (2.0 * math.pi / BOX)
    exact = jnp.concatenate([jnp.cos(angle), jnp.sin(angle)], axis=1)
    high = lax.reduce_precision(exact, 8, 7)
    rest = exact - high
    middle = lax.reduce_precision(rest, 8, 7)
    low = rest - middle
    return jnp.concatenate([high, middle, low, jnp.zeros((128 - 3 * SHIFTS, F), f32)], axis=0).astype(bf16)


def shift_kernel(place_ref, index_ref, table_ref, image_ref, out_ref, send_ref):
    core = place_ref[0]
    index = index_ref[...]
    lane = lax.broadcasted_iota(jnp.int32, (ROW_BLOCK, 128), 1)
    chosen = (lane == index) | (lane == index + SHIFTS) | (lane == index + 2 * SHIFTS)
    chosen = jnp.where(chosen, 1.0, 0.0).astype(bf16)
    for at in range(0, H, 512):
        cosine = jnp.dot(chosen, table_ref[:, at : at + 512], preferred_element_type=f32)
        sine = jnp.dot(chosen, table_ref[:, H + at : H + at + 512], preferred_element_type=f32)
        real = image_ref[:, at : at + 512].astype(f32)
        imag = image_ref[:, H + at : H + at + 512].astype(f32)
        for value, start in ((real * cosine + imag * sine, at // 2), (imag * cosine - real * sine, (H + at) // 2)):
            for m in range(2):
                even = value[:, 256 * m : 256 * m + 128]
                odd = value[:, 256 * m + 128 : 256 * m + 256]
                column = start + 128 * m
                out_ref[:, column : column + 128] = even.astype(bf16)
                out_ref[:, H + column : H + column + 128] = odd.astype(bf16)
                send_ref[:, column : column + 128] = jnp.where(core == 0, odd, even).astype(bf16)


def shift_particles(particles, shift_index, table, place):
    return pl.pallas_call(
        shift_kernel,
        grid=(P_DEV // ROW_BLOCK,),
        in_specs=[
            pl.BlockSpec(memory_space=pltpu.SMEM),
            pl.BlockSpec((ROW_BLOCK, 1), lambda i: (i, 0)),
            pl.BlockSpec((128, F), lambda i: (0, 0)),
            pl.BlockSpec((ROW_BLOCK, F), lambda i: (i, 0)),
        ],
        out_specs=[pl.BlockSpec((ROW_BLOCK, F), lambda i: (i, 0)), pl.BlockSpec((ROW_BLOCK, H), lambda i: (i, 0))],
        out_shape=[pltpu.HBM((P_DEV, F), bf16), pltpu.HBM((P_DEV, H), bf16)],
        compiler_params=pltpu.CompilerParams(vmem_limit_bytes=16 << 20),
        name="shift",
    )(place, shift_index, table, pltpu.with_memory_space_constraint(particles, pltpu.HBM))


def exchange(array, axis):
    return lax.all_to_all(array, axis, 0, 0, tiled=True)


def gather_table(references, particles, shift_index, place):
    mine = references.reshape(K, TILES, 128).transpose(1, 0, 2)
    spread = jnp.broadcast_to(mine, (8, TILES, K, 128))
    along_z = exchange(spread, Z)
    shifted, send = shift_particles(particles, shift_index[:, None], phase_table(), place)
    along_z, shifted, send = lax.optimization_barrier((along_z, shifted, send))
    spread = jnp.broadcast_to(along_z, (4, 8, TILES, K, 128))
    along_y = exchange(spread, "y")
    received = lax.ppermute(send, "c", [(0, 1), (1, 0)])
    other = lax.ppermute(along_y, "c", [(0, 1), (1, 0)])
    return along_y.reshape(8, 4, TILES, K, 128), other.reshape(8, 4, TILES, K, 128), shifted, received


def fill_table(source_ref, table_ref, core):
    for zb in range(4):
        for b in range(3):
            part = 6 * zb + 3 * core + b
            turn = part // 8
            column = (part - 8 * turn) * 256
            rows = pl.ds(pl.multiple_of(turn * 64, 64), 64)
            for lanes in range(4):
                tiles = source_ref[:, zb, 4 * b + lanes].reshape(64, 128)
                start = pl.multiple_of(column + lanes % 2 * H + lanes // 2 * 128, 128)
                table_ref[rows, pl.ds(start, 128)] = tiles


def load_kernel(place_ref, own_ref, shifted_ref, images_ref, table_ref, arrived):
    copies = []
    for q in range(8):
        columns = pl.ds(q * 512, 512)
        copies.append(pltpu.make_async_copy(shifted_ref.at[:, columns], images_ref.at[:, columns], arrived.at[q]))
        copies[-1].start()
    fill_table(own_ref, table_ref, place_ref[0])
    for copy in copies:
        copy.wait()


def load_own(place, own, shifted):
    vmem = pl.BlockSpec(memory_space=pltpu.VMEM)
    return pl.pallas_call(
        load_kernel,
        in_specs=[pl.BlockSpec(memory_space=pltpu.SMEM), vmem, pl.BlockSpec(memory_space=pltpu.HBM)],
        out_specs=[vmem, vmem],
        out_shape=[pltpu.VMEM((P_DEV, F), bf16), pltpu.VMEM((ROWS, F), bf16)],
        scratch_shapes=[pltpu.SemaphoreType.DMA((8,))],
        compiler_params=pltpu.CompilerParams(vmem_limit_bytes=16 << 20),
        name="load",
    )(place, own, pltpu.with_memory_space_constraint(shifted, pltpu.HBM))


def score_kernel(place_ref, other_ref, half_ref, shifted_ref, class_ref, rotation_ref, precision_ref, scores_ref, stats_ref, table_ref):
    fill_table(other_ref, table_ref, 1 - place_ref[0])
    half_norm = jnp.zeros((ROWS, 128), f32)
    for at in range(0, F, 128):
        piece = table_ref[:, at : at + 128].astype(f32)
        half_norm = half_norm + piece * piece
    half_norm = 0.5 * jnp.sum(half_norm, axis=1, keepdims=True)
    correlation = lax.dot_general(table_ref[...], shifted_ref[...], (((1,), (1,)), ((), ())), preferred_element_type=f32)
    row = lax.broadcasted_iota(jnp.int32, (ROWS, 1), 0)
    class_ids = place_ref[1] + row % K
    rotation_ids = (row // K) % 8 * 3 + row // 64
    distance = jnp.abs(rotation_ids - rotation_ref[...])
    distance = jnp.minimum(distance, R - distance).astype(f32)
    width = R / 8.0
    match = jnp.where(class_ids == class_ref[...], 1.0, 0.0)
    scores = precision_ref[...] * (correlation - half_norm) + (-distance * distance / (2.0 * width * width) + match)
    scores_ref[...] = scores
    top = jnp.max(scores, axis=0, keepdims=True)
    mass = jnp.sum(jnp.exp(scores - top), axis=0, keepdims=True)
    for at in range(8):
        stats_ref[at, 0:1, :] = top
        stats_ref[at, 1:2, :] = mass


def local_scores(place, own, other, shifted, prev_class, prev_rotation, precision):
    images, half = load_own(place, own, shifted)
    vmem = pl.BlockSpec(memory_space=pltpu.VMEM)
    scores, stats, _ = pl.pallas_call(
        score_kernel,
        in_specs=[pl.BlockSpec(memory_space=pltpu.SMEM)] + [vmem] * 6,
        out_specs=[vmem, vmem, vmem],
        out_shape=[jax.ShapeDtypeStruct((ROWS, P_DEV), f32), jax.ShapeDtypeStruct((8, 2, P_DEV), f32), pltpu.VMEM((ROWS, F), bf16)],
        input_output_aliases={2: 2},
        compiler_params=pltpu.CompilerParams(vmem_limit_bytes=16 << 20),
        name="scores",
    )(place, other, half, images, prev_class[None, :], prev_rotation[None, :], precision[None, :])
    return scores, stats, images


def weigh_kernel(stats_ref, scores_ref, weights_ref, mass_ref, evidence_ref):
    tops = [stats_ref[i, 0:1, :] for i in range(8)]
    top = tops[0]
    for i in range(1, 8):
        top = jnp.maximum(top, tops[i])
    mass = jnp.zeros_like(top)
    for i in range(8):
        mass = mass + stats_ref[i, 1:2, :] * jnp.exp(tops[i] - top)
    evidence_ref[...] = top + jnp.log(mass)
    probs = jnp.exp(scores_ref[...] - top) * (1.0 / mass)
    weights_ref[...] = probs.astype(bf16)
    occupancy = jnp.sum(probs, axis=1, keepdims=True)
    high = occupancy.astype(bf16).astype(f32)
    low = occupancy - high
    lane = lax.broadcasted_iota(jnp.int32, (4, K, 128), 2)
    tile = jnp.zeros((4, K, 128), f32)
    for za in range(2):
        for turn in range(3):
            rows = slice(64 * turn, 64 * turn + 64)
            spread_high = jnp.broadcast_to(high[rows].reshape(4, 2, K, 1)[:, za], (4, K, 128))
            spread_low = jnp.broadcast_to(low[rows].reshape(4, 2, K, 1)[:, za], (4, K, 128))
            for part in range(8 * turn, 8 * turn + 8):
                at = 6 * (8 * za + part // 3) + part % 3
                tile = jnp.where(lane == at, spread_high, tile)
                tile = jnp.where(lane == at + 3, spread_low, tile)
    mass_ref[...] = tile.astype(bf16)


def weigh(stats, scores):
    vmem = pl.BlockSpec(memory_space=pltpu.VMEM)
    return pl.pallas_call(
        weigh_kernel,
        in_specs=[vmem, vmem],
        out_specs=[vmem, vmem, vmem],
        out_shape=[
            jax.ShapeDtypeStruct((ROWS, P_DEV), bf16),
            jax.ShapeDtypeStruct((4, K, 128), bf16),
            jax.ShapeDtypeStruct((1, P_DEV), f32),
        ],
        compiler_params=pltpu.CompilerParams(vmem_limit_bytes=16 << 20),
        name="weigh",
    )(stats, scores)


def sum_kernel(place_ref, weights_ref, mass_ref, shifted_ref, received_ref, pieces_ref):
    core = place_ref[0]
    own, other = weights_ref[core], weights_ref[1 - core]
    for q in range(8):
        columns = pl.ds(pl.multiple_of(core * H + q * 256, 256), 256)
        numerator = jnp.dot(own, shifted_ref[:, columns], preferred_element_type=f32)
        numerator = numerator + jnp.dot(other, received_ref[:, q * 256 : q * 256 + 256], preferred_element_type=f32)
        for turn in range(3):
            part = 8 * turn + q
            for m in range(2):
                tile = numerator[64 * turn : 64 * turn + 64, 128 * m : 128 * m + 128].reshape(4, 2, K, 128)
                for za in range(2):
                    at = 6 * (8 * za + part // 3) + 2 * (part % 3) + m
                    pieces_ref[:, at] = tile[:, za].astype(bf16)
    pieces_ref[:, PIECES] = mass_ref[...]


def local_sums(place, weights, mass, shifted, received):
    vmem = pl.BlockSpec(memory_space=pltpu.VMEM)
    return pl.pallas_call(
        sum_kernel,
        in_specs=[pl.BlockSpec(memory_space=pltpu.SMEM)] + [vmem] * 4,
        out_specs=vmem,
        out_shape=jax.ShapeDtypeStruct((4, PIECES + 1, K, 128), bf16),
        compiler_params=pltpu.CompilerParams(vmem_limit_bytes=16 << 20),
        name="sums",
    )(place, weights, mass, shifted, received)


def fold_kernel(pieces_ref, out_ref):
    total = pieces_ref[0].astype(f32)
    for i in range(1, 4):
        total = total + pieces_ref[i].astype(f32)
    total = total.astype(bf16)
    for i in range(16):
        out_ref[i, 0:6] = total[6 * i : 6 * i + 6]
        out_ref[i, 6] = total[PIECES]


def finish_kernel(place_ref, pieces_ref, out_ref):
    halves = []
    for half in range(2):
        total = pieces_ref[half].astype(f32)
        for i in range(1, 8):
            total = total + pieces_ref[2 * i + half].astype(f32)
        halves.append(total)
    mass = halves[0][6] + halves[1][6]
    lane = lax.broadcasted_iota(jnp.int32, (K, 128), 1) - 6 * place_ref[2]
    for b in range(3):
        picked = jnp.where((lane == b) | (lane == b + 3), mass, 0.0)
        scale = 1.0 / (jnp.sum(picked, axis=1, keepdims=True) + 1.0)
        for lanes in range(4):
            at = 4 * b + lanes
            out_ref[:, at * 128 : at * 128 + 128] = halves[lanes % 2][2 * b + lanes // 2] * scale


def scatter_sums(place, pieces):
    vmem = pl.BlockSpec(memory_space=pltpu.VMEM)
    params = pltpu.CompilerParams(vmem_limit_bytes=16 << 20)
    pieces = exchange(pieces, "y")
    pieces = pl.pallas_call(
        fold_kernel,
        in_specs=[vmem],
        out_specs=vmem,
        out_shape=jax.ShapeDtypeStruct((16, 7, K, 128), bf16),
        compiler_params=params,
        name="fold",
    )(pieces)
    pieces = exchange(pieces, Z + ("c",))
    return pl.pallas_call(
        finish_kernel,
        in_specs=[pl.BlockSpec(memory_space=pltpu.SMEM), vmem],
        out_specs=vmem,
        out_shape=jax.ShapeDtypeStruct((K, TILES * 128), f32),
        compiler_params=params,
        name="finish",
    )(place, pieces)


def on_device(particles, shift_index, prev_class, prev_rotation, precision, references):
    place = jnp.stack([lax.axis_index("c"), lax.axis_index(CLS) * K, lax.axis_index(Z + ("c",))]).astype(jnp.int32)
    own, other, shifted, received = gather_table(references, particles, shift_index, place)
    scores, stats, images = local_scores(place, own, other, shifted, prev_class, prev_rotation, precision)
    stats = exchange(stats, CLS)
    weights, mass, evidence = weigh(stats, scores)
    weights = lax.all_gather(weights, "c", axis=0)
    pieces = local_sums(place, weights, mass, images, received)
    return (scatter_sums(place, pieces), evidence.reshape(P_DEV))


def solution(mesh):
    split = Mesh(mesh.devices.reshape(4, 2, 4, 2, 2, 4), DOM + CLS)
    return jax.shard_map(
        on_device,
        mesh=split,
        in_specs=(P(DOM, None), P(DOM), P(DOM), P(DOM), P(DOM), P(CLS, DOM)),
        out_specs=(P(CLS, DOM), P(DOM)),
        check_vma=False,
    )
```

```python
import functools
import math

import jax
import jax.numpy as jnp
from jax import lax
from jax.experimental import pallas as pl
from jax.experimental.pallas import tpu as pltpu
from jax.sharding import Mesh
from jax.sharding import PartitionSpec as P

BOX = 64
F = 4096
H = F // 2
R = 24
K = 8
ROWS = K * R
SHIFTS = 25
SIDE = 5
P_DEV = 576
ROW_BLOCK = 96
TILES = 12
PIECES = 96

bf16 = jnp.bfloat16
f32 = jnp.float32

Z = ("za", "zb")
CLS = ("zh", "x")
DOM = ("y", "za", "zb", "c")


def phase_table():
    frequency = jnp.arange(H, dtype=jnp.int32)
    freq_x = frequency % BOX - BOX // 2
    freq_y = frequency // BOX
    shift = jnp.arange(SHIFTS, dtype=jnp.int32)
    step_x = shift % SIDE - 2
    step_y = shift // SIDE - 2
    phase = (freq_x[None, :] * step_x[:, None] + freq_y[None, :] * step_y[:, None]) % BOX
    angle = phase.astype(f32) * (2.0 * math.pi / BOX)
    exact = jnp.concatenate([jnp.cos(angle), jnp.sin(angle)], axis=1)
    high = lax.reduce_precision(exact, 8, 7)
    rest = exact - high
    middle = lax.reduce_precision(rest, 8, 7)
    low = rest - middle
    return jnp.concatenate([high, middle, low, jnp.zeros((128 - 3 * SHIFTS, F), f32)], axis=0).astype(bf16)


def shift_kernel(index_ref, table_ref, image_ref, out_ref):
    index = index_ref[...]
    lane = lax.broadcasted_iota(jnp.int32, (ROW_BLOCK, 128), 1)
    chosen = (lane == index) | (lane == index + SHIFTS) | (lane == index + 2 * SHIFTS)
    chosen = jnp.where(chosen, 1.0, 0.0).astype(bf16)
    for at in range(0, H, 512):
        cosine = jnp.dot(chosen, table_ref[:, at : at + 512], preferred_element_type=f32)
        sine = jnp.dot(chosen, table_ref[:, H + at : H + at + 512], preferred_element_type=f32)
        real = image_ref[:, at : at + 512].astype(f32)
        imag = image_ref[:, H + at : H + at + 512].astype(f32)
        out_ref[:, at : at + 512] = (real * cosine + imag * sine).astype(bf16)
        out_ref[:, H + at : H + at + 512] = (imag * cosine - real * sine).astype(bf16)


def shift_particles(particles, shift_index, table):
    return pl.pallas_call(
        shift_kernel,
        grid=(P_DEV // ROW_BLOCK,),
        in_specs=[
            pl.BlockSpec((ROW_BLOCK, 1), lambda i: (i, 0)),
            pl.BlockSpec((128, F), lambda i: (0, 0)),
            pl.BlockSpec((ROW_BLOCK, F), lambda i: (i, 0)),
        ],
        out_specs=pl.BlockSpec((ROW_BLOCK, F), lambda i: (i, 0)),
        out_shape=pltpu.HBM((P_DEV, F), bf16),
        compiler_params=pltpu.CompilerParams(vmem_limit_bytes=16 << 20),
        name="shift",
    )(shift_index, table, particles)


def exchange(array, axis):
    return lax.all_to_all(array, axis, 0, 0, tiled=True)


def gather_table(references, particles, shift_index):
    mine = references.reshape(K, TILES, 128).transpose(1, 0, 2)
    along_z = exchange(jnp.broadcast_to(mine, (8, TILES, K, 128)), Z)
    along_z, index, phases = lax.optimization_barrier((along_z, shift_index[:, None], phase_table()))
    along_y = exchange(jnp.broadcast_to(along_z, (4, 8, TILES, K, 128)), "y")
    along_y, shifted = lax.optimization_barrier((along_y, shift_particles(particles, index, phases)))
    other = lax.ppermute(along_y, "c", [(0, 1), (1, 0)])
    return along_y.reshape(8, 4, TILES, K, 128), other.reshape(8, 4, TILES, K, 128), shifted


def fill_table(source_ref, table_ref, core):
    for zb in range(4):
        for b in range(3):
            part = 6 * zb + 3 * core + b
            turn = part // 8
            column = (part - 8 * turn) * 512
            rows = pl.ds(pl.multiple_of(turn * 64, 64), 64)
            for lanes in range(4):
                tiles = source_ref[:, zb, 4 * b + lanes].reshape(64, 128)
                table_ref[rows, pl.ds(pl.multiple_of(column + lanes * 128, 128), 128)] = tiles


def load_kernel(place_ref, own_ref, shifted_ref, images_ref, table_ref, arrived):
    copies = []
    for q in range(8):
        columns = pl.ds(q * 512, 512)
        copies.append(pltpu.make_async_copy(shifted_ref.at[:, columns], images_ref.at[:, columns], arrived.at[q]))
        copies[-1].start()
    fill_table(own_ref, table_ref, place_ref[0])
    for copy in copies:
        copy.wait()


def load_own(place, own, shifted):
    vmem = pl.BlockSpec(memory_space=pltpu.VMEM)
    return pl.pallas_call(
        load_kernel,
        in_specs=[pl.BlockSpec(memory_space=pltpu.SMEM), vmem, pl.BlockSpec(memory_space=pltpu.HBM)],
        out_specs=[vmem, vmem],
        out_shape=[pltpu.VMEM((P_DEV, F), bf16), pltpu.VMEM((ROWS, F), bf16)],
        scratch_shapes=[pltpu.SemaphoreType.DMA((8,))],
        compiler_params=pltpu.CompilerParams(vmem_limit_bytes=16 << 20),
        name="load",
    )(place, own, pltpu.with_memory_space_constraint(shifted, pltpu.HBM))


def score_kernel(place_ref, other_ref, half_ref, shifted_ref, class_ref, rotation_ref, precision_ref, scores_ref, stats_ref, table_ref):
    fill_table(other_ref, table_ref, 1 - place_ref[0])
    half_norm = jnp.zeros((ROWS, 128), f32)
    for at in range(0, F, 128):
        piece = table_ref[:, at : at + 128].astype(f32)
        half_norm = half_norm + piece * piece
    half_norm = 0.5 * jnp.sum(half_norm, axis=1, keepdims=True)
    correlation = lax.dot_general(table_ref[...], shifted_ref[...], (((1,), (1,)), ((), ())), preferred_element_type=f32)
    row = lax.broadcasted_iota(jnp.int32, (ROWS, 1), 0)
    class_ids = place_ref[1] + row % K
    rotation_ids = (row // K) % 8 * 3 + row // 64
    distance = jnp.abs(rotation_ids - rotation_ref[...])
    distance = jnp.minimum(distance, R - distance).astype(f32)
    width = R / 8.0
    match = jnp.where(class_ids == class_ref[...], 1.0, 0.0)
    scores = precision_ref[...] * (correlation - half_norm) + (-distance * distance / (2.0 * width * width) + match)
    scores_ref[...] = scores
    top = jnp.max(scores, axis=0, keepdims=True)
    mass = jnp.sum(jnp.exp(scores - top), axis=0, keepdims=True)
    for at in range(8):
        stats_ref[at, 0:1, :] = top
        stats_ref[at, 1:2, :] = mass


def local_scores(place, own, other, shifted, prev_class, prev_rotation, precision):
    images, half = load_own(place, own, shifted)
    vmem = pl.BlockSpec(memory_space=pltpu.VMEM)
    scores, stats, _ = pl.pallas_call(
        score_kernel,
        in_specs=[pl.BlockSpec(memory_space=pltpu.SMEM)] + [vmem] * 6,
        out_specs=[vmem, vmem, vmem],
        out_shape=[jax.ShapeDtypeStruct((ROWS, P_DEV), f32), jax.ShapeDtypeStruct((8, 2, P_DEV), f32), pltpu.VMEM((ROWS, F), bf16)],
        input_output_aliases={2: 2},
        compiler_params=pltpu.CompilerParams(vmem_limit_bytes=16 << 20),
        name="scores",
    )(place, other, half, images, prev_class[None, :], prev_rotation[None, :], precision[None, :])
    return scores, stats, images


def sum_kernel(place_ref, stats_ref, scores_ref, shifted_ref, keep_ref, send_ref, evidence_ref):
    tops = [stats_ref[i, 0:1, :] for i in range(8)]
    top = tops[0]
    for i in range(1, 8):
        top = jnp.maximum(top, tops[i])
    mass = jnp.zeros_like(top)
    for i in range(8):
        mass = mass + stats_ref[i, 1:2, :] * jnp.exp(tops[i] - top)
    evidence_ref[...] = (top + jnp.log(mass)).reshape(P_DEV)
    probs = jnp.exp(scores_ref[...] - top) * (1.0 / mass)
    weights = probs.astype(bf16)
    occupancy = jnp.sum(probs, axis=1, keepdims=True)
    high = occupancy.astype(bf16).astype(f32)
    low = occupancy - high
    lane = lax.broadcasted_iota(jnp.int32, (4, K, 128), 2)
    masses = [jnp.zeros((4, K, 128), f32), jnp.zeros((4, K, 128), f32)]
    for za in range(2):
        for turn in range(3):
            rows = slice(64 * turn, 64 * turn + 64)
            spread_high = jnp.broadcast_to(high[rows].reshape(4, 2, K, 1)[:, za], (4, K, 128))
            spread_low = jnp.broadcast_to(low[rows].reshape(4, 2, K, 1)[:, za], (4, K, 128))
            for part in range(8 * turn, 8 * turn + 8):
                zb, to, b = part // 6, part // 3 % 2, part % 3
                at = 6 * (4 * za + zb) + b
                masses[to] = jnp.where(lane == at, spread_high, masses[to])
                masses[to] = jnp.where(lane == at + 3, spread_low, masses[to])

    def pack(core):
        for q in range(8):
            numerator = jnp.dot(weights, shifted_ref[:, q * 512 : q * 512 + 512], preferred_element_type=f32)
            for turn in range(3):
                part = 8 * turn + q
                zb, to, b = part // 6, part // 3 % 2, part % 3
                for lanes in range(4):
                    tile = numerator[64 * turn : 64 * turn + 64, 128 * lanes : 128 * lanes + 128].reshape(4, 2, K, 128)
                    for za in range(2):
                        at = 12 * (4 * za + zb) + 4 * b + lanes
                        if to == core:
                            keep_ref[:, at] = tile[:, za]
                        else:
                            send_ref[:, at] = tile[:, za].astype(bf16)
        keep_ref[:, PIECES] = masses[core]
        send_ref[:, PIECES] = masses[1 - core].astype(bf16)

    for core in range(2):
        pl.when(place_ref[0] == core)(functools.partial(pack, core))


def local_sums(place, stats, scores, shifted):
    vmem = pl.BlockSpec(memory_space=pltpu.VMEM)
    return pl.pallas_call(
        sum_kernel,
        in_specs=[pl.BlockSpec(memory_space=pltpu.SMEM)] + [vmem] * 3,
        out_specs=[vmem, vmem, vmem],
        out_shape=[
            jax.ShapeDtypeStruct((4, PIECES + 1, K, 128), f32),
            jax.ShapeDtypeStruct((4, PIECES + 1, K, 128), bf16),
            jax.ShapeDtypeStruct((P_DEV,), f32),
        ],
        compiler_params=pltpu.CompilerParams(vmem_limit_bytes=16 << 20),
        name="sums",
    )(place, stats, scores, shifted)


def fold_kernel(pieces_ref, out_ref):
    total = pieces_ref[0].astype(f32)
    for i in range(1, 4):
        total = total + pieces_ref[i].astype(f32)
    total = total.astype(bf16)
    for i in range(8):
        out_ref[i, 0:TILES] = total[TILES * i : TILES * i + TILES]
        out_ref[i, TILES] = total[PIECES]


def finish_kernel(place_ref, pieces_ref, out_ref):
    total = pieces_ref[0].astype(f32)
    for i in range(1, 8):
        total = total + pieces_ref[i].astype(f32)
    lane = lax.broadcasted_iota(jnp.int32, (K, 128), 1) - 6 * place_ref[2]
    for b in range(3):
        picked = jnp.where((lane == b) | (lane == b + 3), total[TILES], 0.0)
        scale = 1.0 / (jnp.sum(picked, axis=1, keepdims=True) + 1.0)
        for lanes in range(4):
            at = 4 * b + lanes
            out_ref[:, at * 128 : at * 128 + 128] = total[at] * scale


def scatter_sums(place, keep, send):
    vmem = pl.BlockSpec(memory_space=pltpu.VMEM)
    params = pltpu.CompilerParams(vmem_limit_bytes=16 << 20)
    received = lax.ppermute(send, "c", [(0, 1), (1, 0)])
    pieces = exchange((keep + received.astype(f32)).astype(bf16), "y")
    pieces = pl.pallas_call(
        fold_kernel,
        in_specs=[vmem],
        out_specs=vmem,
        out_shape=jax.ShapeDtypeStruct((8, TILES + 1, K, 128), bf16),
        compiler_params=params,
        name="fold",
    )(pieces)
    pieces = exchange(pieces, Z)
    return pl.pallas_call(
        finish_kernel,
        in_specs=[pl.BlockSpec(memory_space=pltpu.SMEM), vmem],
        out_specs=vmem,
        out_shape=jax.ShapeDtypeStruct((K, TILES * 128), f32),
        compiler_params=params,
        name="finish",
    )(place, pieces)


def on_device(particles, shift_index, prev_class, prev_rotation, precision, references):
    place = jnp.stack([lax.axis_index("c"), lax.axis_index(CLS) * K, lax.axis_index(Z)]).astype(jnp.int32)
    own, other, shifted = gather_table(references, particles, shift_index)
    scores, stats, images = local_scores(place, own, other, shifted, prev_class, prev_rotation, precision)
    stats = exchange(stats, CLS)
    keep, send, evidence = local_sums(place, stats, scores, images)
    return (scatter_sums(place, keep, send), evidence)


def solution(mesh):
    split = Mesh(mesh.devices.reshape(4, 2, 4, 2, 2, 4), DOM + CLS)
    return jax.shard_map(
        on_device,
        mesh=split,
        in_specs=(P(DOM, None), P(DOM), P(DOM), P(DOM), P(DOM), P(CLS, DOM)),
        out_specs=(P(CLS, DOM), P(DOM)),
        check_vma=False,
    )
```

```python
import math

import jax
import jax.numpy as jnp
import ml_dtypes
import numpy as np
from jax import lax
from jax.experimental import pallas as pl
from jax.experimental.pallas import tpu as pltpu
from jax.sharding import Mesh
from jax.sharding import PartitionSpec as P

BOX = 64
F = 4096
H = F // 2
R = 24
K = 8
ROWS = K * R
SHIFTS = 25
SIDE = 5
P_DEV = 576
ROW_BLOCK = 288
TILES = 12
PIECES = 96

bf16 = jnp.bfloat16
f32 = jnp.float32

Z = ("za", "zb")
CLS = ("zh", "x")
DOM = ("y", "za", "zb", "c")


def phase_table():
    frequency = np.arange(H)
    shift = np.arange(SHIFTS)
    step_x, step_y = shift % SIDE - 2, shift // SIDE - 2
    phase = (np.outer(step_x, frequency % BOX - BOX // 2) + np.outer(step_y, frequency // BOX)) % BOX
    angle = phase * (2.0 * math.pi / BOX)
    rest = np.concatenate([np.cos(angle), np.sin(angle)], axis=1).astype(np.float32)
    terms = []
    for _ in range(3):
        terms.append(rest.astype(ml_dtypes.bfloat16))
        rest = rest - terms[-1].astype(np.float32)
    terms.append(np.zeros((128 - 3 * SHIFTS, F), ml_dtypes.bfloat16))
    return jnp.asarray(np.concatenate(terms, axis=0))


def shift_kernel(index_ref, table_ref, image_ref, out_ref):
    index = index_ref[...]
    lane = lax.broadcasted_iota(jnp.int32, (ROW_BLOCK, 128), 1)
    chosen = (lane == index) | (lane == index + SHIFTS) | (lane == index + 2 * SHIFTS)
    chosen = jnp.where(chosen, 1.0, 0.0).astype(bf16)
    for at in range(0, H, 512):
        cosine = jnp.dot(chosen, table_ref[:, at : at + 512], preferred_element_type=f32)
        sine = jnp.dot(chosen, table_ref[:, H + at : H + at + 512], preferred_element_type=f32)
        real = image_ref[:, at : at + 512].astype(f32)
        imag = image_ref[:, H + at : H + at + 512].astype(f32)
        out_ref[:, at : at + 512] = (real * cosine + imag * sine).astype(bf16)
        out_ref[:, H + at : H + at + 512] = (imag * cosine - real * sine).astype(bf16)


def shift_particles(particles, shift_index, table):
    return pl.pallas_call(
        shift_kernel,
        grid=(P_DEV // ROW_BLOCK,),
        in_specs=[
            pl.BlockSpec((ROW_BLOCK, 1), lambda i: (i, 0)),
            pl.BlockSpec((128, F), lambda i: (0, 0)),
            pl.BlockSpec((ROW_BLOCK, F), lambda i: (i, 0)),
        ],
        out_specs=pl.BlockSpec((ROW_BLOCK, F), lambda i: (i, 0)),
        out_shape=pltpu.HBM((P_DEV, F), bf16),
        compiler_params=pltpu.CompilerParams(vmem_limit_bytes=16 << 20),
        name="shift",
    )(shift_index, table, pltpu.with_memory_space_constraint(particles, pltpu.HBM))


def exchange(array, axis):
    return lax.all_to_all(array, axis, 0, 0, tiled=True)


def gather_table(references, particles, shift_index):
    mine = references.reshape(K, TILES, 128).transpose(1, 0, 2)
    along_z = exchange(jnp.broadcast_to(mine, (8, TILES, K, 128)), Z)
    along_z, index = lax.optimization_barrier((along_z, shift_index))
    along_y = exchange(jnp.broadcast_to(along_z, (4, 8, TILES, K, 128)), "y")
    along_y, shifted = lax.optimization_barrier((along_y, shift_particles(particles, index[:, None], phase_table())))
    other = lax.ppermute(along_y, "c", [(0, 1), (1, 0)])
    return along_y.reshape(8, 4, TILES, K, 128), other.reshape(8, 4, TILES, K, 128), shifted


def fill_table(source_ref, table_ref, core):
    for zb in range(4):
        for b in range(3):
            part = 6 * zb + 3 * core + b
            turn = part // 8
            column = (part - 8 * turn) * 512
            rows = pl.ds(pl.multiple_of(turn * 64, 64), 64)
            for lanes in range(4):
                tiles = source_ref[:, zb, 4 * b + lanes].reshape(64, 128)
                table_ref[rows, pl.ds(pl.multiple_of(column + lanes * 128, 128), 128)] = tiles


def load_kernel(place_ref, own_ref, shifted_ref, images_ref, table_ref, arrived):
    copies = []
    for q in range(8):
        columns = pl.ds(q * 512, 512)
        copies.append(pltpu.make_async_copy(shifted_ref.at[:, columns], images_ref.at[:, columns], arrived.at[q]))
        copies[-1].start()
    fill_table(own_ref, table_ref, place_ref[0])
    for copy in copies:
        copy.wait()


def load_own(place, own, shifted):
    vmem = pl.BlockSpec(memory_space=pltpu.VMEM)
    return pl.pallas_call(
        load_kernel,
        in_specs=[pl.BlockSpec(memory_space=pltpu.SMEM), vmem, pl.BlockSpec(memory_space=pltpu.HBM)],
        out_specs=[vmem, vmem],
        out_shape=[pltpu.VMEM((P_DEV, F), bf16), pltpu.VMEM((ROWS, F), bf16)],
        scratch_shapes=[pltpu.SemaphoreType.DMA((8,))],
        compiler_params=pltpu.CompilerParams(vmem_limit_bytes=16 << 20),
        name="load",
    )(place, own, pltpu.with_memory_space_constraint(shifted, pltpu.HBM))


def score_kernel(place_ref, other_ref, half_ref, shifted_ref, class_ref, rotation_ref, precision_ref, scores_ref, stats_ref, table_ref):
    fill_table(other_ref, table_ref, 1 - place_ref[0])
    half_norm = jnp.zeros((ROWS, 128), f32)
    for at in range(0, F, 128):
        piece = table_ref[:, at : at + 128].astype(f32)
        half_norm = half_norm + piece * piece
    half_norm = 0.5 * jnp.sum(half_norm, axis=1, keepdims=True)
    correlation = lax.dot_general(table_ref[...], shifted_ref[...], (((1,), (1,)), ((), ())), preferred_element_type=f32)
    row = lax.broadcasted_iota(jnp.int32, (ROWS, 1), 0)
    class_ids = place_ref[1] + row % K
    rotation_ids = (row // K) % 8 * 3 + row // 64
    distance = jnp.abs(rotation_ids - rotation_ref[...])
    distance = jnp.minimum(distance, R - distance).astype(f32)
    width = R / 8.0
    match = jnp.where(class_ids == class_ref[...], 1.0, 0.0)
    scores = precision_ref[...] * (correlation - half_norm) + (-distance * distance / (2.0 * width * width) + match)
    scores_ref[...] = scores
    top = jnp.max(scores, axis=0, keepdims=True)
    mass = jnp.sum(jnp.exp(scores - top), axis=0, keepdims=True)
    for at in range(8):
        stats_ref[at, 0:1, :] = top
        stats_ref[at, 1:2, :] = mass


def local_scores(place, own, other, shifted, prev_class, prev_rotation, precision):
    images, half = load_own(place, own, shifted)
    vmem = pl.BlockSpec(memory_space=pltpu.VMEM)
    scores, stats, _ = pl.pallas_call(
        score_kernel,
        in_specs=[pl.BlockSpec(memory_space=pltpu.SMEM)] + [vmem] * 6,
        out_specs=[vmem, vmem, vmem],
        out_shape=[jax.ShapeDtypeStruct((ROWS, P_DEV), f32), jax.ShapeDtypeStruct((8, 2, P_DEV), f32), pltpu.VMEM((ROWS, F), bf16)],
        input_output_aliases={2: 2},
        compiler_params=pltpu.CompilerParams(vmem_limit_bytes=16 << 20),
        name="scores",
    )(place, other, half, images, prev_class[None, :], prev_rotation[None, :], precision[None, :])
    return scores, stats, images


def sum_kernel(place_ref, stats_ref, scores_ref, shifted_ref, keep_ref, send_ref, evidence_ref):
    tops = [stats_ref[i, 0:1, :] for i in range(8)]
    top = tops[0]
    for i in range(1, 8):
        top = jnp.maximum(top, tops[i])
    mass = jnp.zeros_like(top)
    for i in range(8):
        mass = mass + stats_ref[i, 1:2, :] * jnp.exp(tops[i] - top)
    evidence_ref[...] = (top + jnp.log(mass)).reshape(P_DEV)
    probs = jnp.exp(scores_ref[...] - top) * (1.0 / mass)
    weights = probs.astype(bf16)
    occupancy = jnp.sum(probs, axis=1, keepdims=True)
    high = occupancy.astype(bf16).astype(f32)
    low = occupancy - high
    lane = lax.broadcasted_iota(jnp.int32, (4, K, 128), 2)
    masses = [jnp.zeros((4, K, 128), f32), jnp.zeros((4, K, 128), f32)]
    for za in range(2):
        for turn in range(3):
            rows = slice(64 * turn, 64 * turn + 64)
            spread_high = jnp.broadcast_to(high[rows].reshape(4, 2, K, 1)[:, za], (4, K, 128))
            spread_low = jnp.broadcast_to(low[rows].reshape(4, 2, K, 1)[:, za], (4, K, 128))
            for part in range(8 * turn, 8 * turn + 8):
                zb, to, b = part // 6, part // 3 % 2, part % 3
                at = 6 * (4 * za + zb) + b
                masses[to] = jnp.where(lane == at, spread_high, masses[to])
                masses[to] = jnp.where(lane == at + 3, spread_low, masses[to])

    swap = place_ref[0] == 1
    numerators = {}
    for q in range(8):
        numerator = jnp.dot(weights, shifted_ref[:, q * 512 : q * 512 + 512], preferred_element_type=f32)
        for turn in range(3):
            numerators[8 * turn + q] = numerator[64 * turn : 64 * turn + 64]
    for part in range(24):
        if part // 3 % 2:
            continue
        zb, b = part // 6, part % 3
        first, second = numerators[part], numerators[part + 3]
        keep = jnp.where(swap, second, first)
        send = jnp.where(swap, first, second)
        for lanes in range(4):
            columns = slice(128 * lanes, 128 * lanes + 128)
            for za in range(2):
                at = 12 * (4 * za + zb) + 4 * b + lanes
                keep_ref[:, at] = keep[:, columns].reshape(4, 2, K, 128)[:, za]
                send_ref[:, at] = send[:, columns].reshape(4, 2, K, 128)[:, za].astype(bf16)
    keep_ref[:, PIECES] = jnp.where(swap, masses[1], masses[0])
    send_ref[:, PIECES] = jnp.where(swap, masses[0], masses[1]).astype(bf16)


def local_sums(place, stats, scores, shifted):
    vmem = pl.BlockSpec(memory_space=pltpu.VMEM)
    return pl.pallas_call(
        sum_kernel,
        in_specs=[pl.BlockSpec(memory_space=pltpu.SMEM)] + [vmem] * 3,
        out_specs=[vmem, vmem, vmem],
        out_shape=[
            jax.ShapeDtypeStruct((4, PIECES + 1, K, 128), f32),
            jax.ShapeDtypeStruct((4, PIECES + 1, K, 128), bf16),
            jax.ShapeDtypeStruct((P_DEV,), f32),
        ],
        compiler_params=pltpu.CompilerParams(vmem_limit_bytes=16 << 20),
        name="sums",
    )(place, stats, scores, shifted)


def fold_kernel(pieces_ref, out_ref):
    total = pieces_ref[0].astype(f32)
    for i in range(1, 4):
        total = total + pieces_ref[i].astype(f32)
    total = total.astype(bf16)
    for i in range(8):
        out_ref[i, 0:TILES] = total[TILES * i : TILES * i + TILES]
        out_ref[i, TILES] = total[PIECES]


def finish_kernel(place_ref, pieces_ref, out_ref):
    total = pieces_ref[0].astype(f32)
    for i in range(1, 8):
        total = total + pieces_ref[i].astype(f32)
    lane = lax.broadcasted_iota(jnp.int32, (K, 128), 1) - 6 * place_ref[2]
    for b in range(3):
        picked = jnp.where((lane == b) | (lane == b + 3), total[TILES], 0.0)
        scale = 1.0 / (jnp.sum(picked, axis=1, keepdims=True) + 1.0)
        for lanes in range(4):
            at = 4 * b + lanes
            out_ref[:, at * 128 : at * 128 + 128] = total[at] * scale


def scatter_sums(place, keep, send):
    vmem = pl.BlockSpec(memory_space=pltpu.VMEM)
    params = pltpu.CompilerParams(vmem_limit_bytes=16 << 20)
    received = lax.ppermute(send, "c", [(0, 1), (1, 0)])
    pieces = exchange((keep + received.astype(f32)).astype(bf16), "y")
    pieces = pl.pallas_call(
        fold_kernel,
        in_specs=[vmem],
        out_specs=vmem,
        out_shape=jax.ShapeDtypeStruct((8, TILES + 1, K, 128), bf16),
        compiler_params=params,
        name="fold",
    )(pieces)
    pieces = exchange(pieces, Z)
    return pl.pallas_call(
        finish_kernel,
        in_specs=[pl.BlockSpec(memory_space=pltpu.SMEM), vmem],
        out_specs=vmem,
        out_shape=jax.ShapeDtypeStruct((K, TILES * 128), f32),
        compiler_params=params,
        name="finish",
    )(place, pieces)


def on_device(particles, shift_index, prev_class, prev_rotation, precision, references):
    place = jnp.stack([lax.axis_index("c"), lax.axis_index(CLS) * K, lax.axis_index(Z)]).astype(jnp.int32)
    own, other, shifted = gather_table(references, particles, shift_index)
    scores, stats, images = local_scores(place, own, other, shifted, prev_class, prev_rotation, precision)
    stats = exchange(stats, CLS)
    keep, send, evidence = local_sums(place, stats, scores, images)
    return (scatter_sums(place, keep, send), evidence)


def solution(mesh):
    split = Mesh(mesh.devices.reshape(4, 2, 4, 2, 2, 4), DOM + CLS)
    return jax.shard_map(
        on_device,
        mesh=split,
        in_specs=(P(DOM, None), P(DOM), P(DOM), P(DOM), P(DOM), P(CLS, DOM)),
        out_specs=(P(CLS, DOM), P(DOM)),
        check_vma=False,
    )
```

```python
import math

import jax
import jax.numpy as jnp
import ml_dtypes
import numpy as np
from jax import lax
from jax.experimental import pallas as pl
from jax.experimental.pallas import tpu as pltpu
from jax.sharding import Mesh
from jax.sharding import PartitionSpec as P

BOX = 64
F = 4096
H = F // 2
R = 24
K = 8
ROWS = K * R
SHIFTS = 25
SIDE = 5
P_DEV = 576
ROW_BLOCK = 288
TILES = 12
PIECES = 96

bf16 = jnp.bfloat16
f32 = jnp.float32

Z = ("za", "zb")
CLS = ("zh", "x")
DOM = ("y", "za", "zb", "c")


def phase_table():
    frequency = np.arange(H)
    shift = np.arange(SHIFTS)
    step_x, step_y = shift % SIDE - 2, shift // SIDE - 2
    phase = (np.outer(step_x, frequency % BOX - BOX // 2) + np.outer(step_y, frequency // BOX)) % BOX
    angle = phase * (2.0 * math.pi / BOX)
    rest = np.concatenate([np.cos(angle), np.sin(angle)], axis=1).astype(np.float32)
    terms = []
    for _ in range(3):
        terms.append(rest.astype(ml_dtypes.bfloat16))
        rest = rest - terms[-1].astype(np.float32)
    terms.append(np.zeros((128 - 3 * SHIFTS, F), ml_dtypes.bfloat16))
    return jnp.asarray(np.concatenate(terms, axis=0))


def shift_kernel(index_ref, table_ref, image_ref, out_ref):
    index = index_ref[...]
    lane = lax.broadcasted_iota(jnp.int32, (ROW_BLOCK, 128), 1)
    chosen = (lane == index) | (lane == index + SHIFTS) | (lane == index + 2 * SHIFTS)
    chosen = jnp.where(chosen, 1.0, 0.0).astype(bf16)
    for at in range(0, H, 512):
        cosine = jnp.dot(chosen, table_ref[:, at : at + 512], preferred_element_type=f32)
        sine = jnp.dot(chosen, table_ref[:, H + at : H + at + 512], preferred_element_type=f32)
        real = image_ref[:, at : at + 512].astype(f32)
        imag = image_ref[:, H + at : H + at + 512].astype(f32)
        out_ref[:, at : at + 512] = (real * cosine + imag * sine).astype(bf16)
        out_ref[:, H + at : H + at + 512] = (imag * cosine - real * sine).astype(bf16)


def shift_particles(particles, shift_index, table):
    return pl.pallas_call(
        shift_kernel,
        grid=(P_DEV // ROW_BLOCK,),
        in_specs=[
            pl.BlockSpec((ROW_BLOCK, 1), lambda i: (i, 0)),
            pl.BlockSpec((128, F), lambda i: (0, 0)),
            pl.BlockSpec((ROW_BLOCK, F), lambda i: (i, 0)),
        ],
        out_specs=pl.BlockSpec((ROW_BLOCK, F), lambda i: (i, 0)),
        out_shape=pltpu.HBM((P_DEV, F), bf16),
        compiler_params=pltpu.CompilerParams(vmem_limit_bytes=16 << 20),
        name="shift",
    )(shift_index, table, pltpu.with_memory_space_constraint(particles, pltpu.HBM))


def exchange(array, axis):
    return lax.all_to_all(array, axis, 0, 0, tiled=True)


def gather_table(references, particles, shift_index):
    mine = references.reshape(K, TILES, 128).transpose(1, 0, 2)
    along_z = exchange(jnp.broadcast_to(mine, (8, TILES, K, 128)), Z)
    along_z, index = lax.optimization_barrier((along_z, shift_index))
    along_y = exchange(jnp.broadcast_to(along_z, (4, 8, TILES, K, 128)), "y")
    along_y, shifted = lax.optimization_barrier((along_y, shift_particles(particles, index[:, None], phase_table())))
    other = lax.ppermute(along_y, "c", [(0, 1), (1, 0)])
    return along_y.reshape(8, 4, TILES, K, 128), other.reshape(8, 4, TILES, K, 128), shifted


def fill_table(source_ref, table_ref, core):
    for zb in range(4):
        for b in range(3):
            part = 6 * zb + 3 * core + b
            turn = part // 8
            column = (part - 8 * turn) * 512
            rows = pl.ds(pl.multiple_of(turn * 64, 64), 64)
            for lanes in range(4):
                tiles = source_ref[:, zb, 4 * b + lanes].reshape(64, 128)
                table_ref[rows, pl.ds(pl.multiple_of(column + lanes * 128, 128), 128)] = tiles


def load_kernel(own_ref, shifted_ref, images_ref, table_ref, arrived):
    copies = []
    for q in range(8):
        columns = pl.ds(q * 512, 512)
        copies.append(pltpu.make_async_copy(shifted_ref.at[:, columns], images_ref.at[:, columns], arrived.at[q]))
        copies[-1].start()
    fill_table(own_ref, table_ref, lax.axis_index("c"))
    for copy in copies:
        copy.wait()


def load_own(own, shifted):
    vmem = pl.BlockSpec(memory_space=pltpu.VMEM)
    return pl.pallas_call(
        load_kernel,
        in_specs=[vmem, pl.BlockSpec(memory_space=pltpu.HBM)],
        out_specs=[vmem, vmem],
        out_shape=[pltpu.VMEM((P_DEV, F), bf16), pltpu.VMEM((ROWS, F), bf16)],
        scratch_shapes=[pltpu.SemaphoreType.DMA((8,))],
        compiler_params=pltpu.CompilerParams(vmem_limit_bytes=16 << 20),
        name="load",
    )(own, pltpu.with_memory_space_constraint(shifted, pltpu.HBM))


def score_kernel(other_ref, half_ref, shifted_ref, class_ref, rotation_ref, precision_ref, scores_ref, stats_ref, table_ref):
    fill_table(other_ref, table_ref, 1 - lax.axis_index("c"))
    half_norm = jnp.zeros((ROWS, 128), f32)
    for at in range(0, F, 128):
        piece = table_ref[:, at : at + 128].astype(f32)
        half_norm = half_norm + piece * piece
    half_norm = 0.5 * jnp.sum(half_norm, axis=1, keepdims=True)
    correlation = lax.dot_general(table_ref[...], shifted_ref[...], (((1,), (1,)), ((), ())), preferred_element_type=f32)
    row = lax.broadcasted_iota(jnp.int32, (ROWS, 1), 0)
    class_ids = lax.axis_index(CLS) * K + row % K
    rotation_ids = (row // K) % 8 * 3 + row // 64
    distance = jnp.abs(rotation_ids - rotation_ref[...])
    distance = jnp.minimum(distance, R - distance).astype(f32)
    width = R / 8.0
    match = jnp.where(class_ids == class_ref[...], 1.0, 0.0)
    scores = precision_ref[...] * (correlation - half_norm) + (-distance * distance / (2.0 * width * width) + match)
    scores_ref[...] = scores
    top = jnp.max(scores, axis=0, keepdims=True)
    mass = jnp.sum(jnp.exp(scores - top), axis=0, keepdims=True)
    for at in range(8):
        stats_ref[at, 0:1, :] = top
        stats_ref[at, 1:2, :] = mass


def local_scores(own, other, shifted, prev_class, prev_rotation, precision):
    images, half = load_own(own, shifted)
    vmem = pl.BlockSpec(memory_space=pltpu.VMEM)
    scores, stats, _ = pl.pallas_call(
        score_kernel,
        in_specs=[vmem] * 6,
        out_specs=[vmem, vmem, vmem],
        out_shape=[jax.ShapeDtypeStruct((ROWS, P_DEV), f32), jax.ShapeDtypeStruct((8, 2, P_DEV), f32), pltpu.VMEM((ROWS, F), bf16)],
        input_output_aliases={1: 2},
        compiler_params=pltpu.CompilerParams(vmem_limit_bytes=16 << 20),
        name="scores",
    )(other, half, images, prev_class[None, :], prev_rotation[None, :], precision[None, :])
    return scores, stats, images


def sum_kernel(stats_ref, scores_ref, shifted_ref, keep_ref, send_ref, evidence_ref):
    tops = [stats_ref[i, 0:1, :] for i in range(8)]
    top = tops[0]
    for i in range(1, 8):
        top = jnp.maximum(top, tops[i])
    mass = jnp.zeros_like(top)
    for i in range(8):
        mass = mass + stats_ref[i, 1:2, :] * jnp.exp(tops[i] - top)
    evidence_ref[...] = (top + jnp.log(mass)).reshape(P_DEV)
    probs = jnp.exp(scores_ref[...] - top) * (1.0 / mass)
    weights = probs.astype(bf16)
    occupancy = jnp.sum(probs, axis=1, keepdims=True)
    high = occupancy.astype(bf16).astype(f32)
    low = occupancy - high
    lane = lax.broadcasted_iota(jnp.int32, (4, K, 128), 2)
    masses = [jnp.zeros((4, K, 128), f32), jnp.zeros((4, K, 128), f32)]
    for za in range(2):
        for turn in range(3):
            rows = slice(64 * turn, 64 * turn + 64)
            spread_high = jnp.broadcast_to(high[rows].reshape(4, 2, K, 1)[:, za], (4, K, 128))
            spread_low = jnp.broadcast_to(low[rows].reshape(4, 2, K, 1)[:, za], (4, K, 128))
            for part in range(8 * turn, 8 * turn + 8):
                zb, to, b = part // 6, part // 3 % 2, part % 3
                at = 6 * (4 * za + zb) + b
                masses[to] = jnp.where(lane == at, spread_high, masses[to])
                masses[to] = jnp.where(lane == at + 3, spread_low, masses[to])

    swap = lax.axis_index("c") == 1
    numerators = {}
    for q in range(8):
        numerator = jnp.dot(weights, shifted_ref[:, q * 512 : q * 512 + 512], preferred_element_type=f32)
        for turn in range(3):
            numerators[8 * turn + q] = numerator[64 * turn : 64 * turn + 64]
    for part in range(24):
        if part // 3 % 2:
            continue
        zb, b = part // 6, part % 3
        first, second = numerators[part], numerators[part + 3]
        keep = jnp.where(swap, second, first)
        send = jnp.where(swap, first, second)
        for lanes in range(4):
            columns = slice(128 * lanes, 128 * lanes + 128)
            for za in range(2):
                at = 12 * (4 * za + zb) + 4 * b + lanes
                keep_ref[:, at] = keep[:, columns].reshape(4, 2, K, 128)[:, za]
                send_ref[:, at] = send[:, columns].reshape(4, 2, K, 128)[:, za].astype(bf16)
    keep_ref[:, PIECES] = jnp.where(swap, masses[1], masses[0])
    send_ref[:, PIECES] = jnp.where(swap, masses[0], masses[1]).astype(bf16)


def local_sums(stats, scores, shifted):
    vmem = pl.BlockSpec(memory_space=pltpu.VMEM)
    return pl.pallas_call(
        sum_kernel,
        in_specs=[vmem] * 3,
        out_specs=[vmem, vmem, vmem],
        out_shape=[
            jax.ShapeDtypeStruct((4, PIECES + 1, K, 128), f32),
            jax.ShapeDtypeStruct((4, PIECES + 1, K, 128), bf16),
            jax.ShapeDtypeStruct((P_DEV,), f32),
        ],
        compiler_params=pltpu.CompilerParams(vmem_limit_bytes=16 << 20),
        name="sums",
    )(stats, scores, shifted)


def fold_kernel(pieces_ref, out_ref):
    total = pieces_ref[0].astype(f32)
    for i in range(1, 4):
        total = total + pieces_ref[i].astype(f32)
    total = total.astype(bf16)
    for i in range(8):
        out_ref[i, 0:TILES] = total[TILES * i : TILES * i + TILES]
        out_ref[i, TILES] = total[PIECES]


def finish_kernel(pieces_ref, out_ref):
    total = pieces_ref[0].astype(f32)
    for i in range(1, 8):
        total = total + pieces_ref[i].astype(f32)
    lane = lax.broadcasted_iota(jnp.int32, (K, 128), 1) - 6 * lax.axis_index(Z)
    for b in range(3):
        picked = jnp.where((lane == b) | (lane == b + 3), total[TILES], 0.0)
        scale = 1.0 / (jnp.sum(picked, axis=1, keepdims=True) + 1.0)
        for lanes in range(4):
            at = 4 * b + lanes
            out_ref[:, at * 128 : at * 128 + 128] = total[at] * scale


def scatter_sums(keep, send):
    vmem = pl.BlockSpec(memory_space=pltpu.VMEM)
    params = pltpu.CompilerParams(vmem_limit_bytes=16 << 20)
    received = lax.ppermute(send, "c", [(0, 1), (1, 0)])
    pieces = exchange((keep + received.astype(f32)).astype(bf16), "y")
    pieces = pl.pallas_call(
        fold_kernel,
        in_specs=[vmem],
        out_specs=vmem,
        out_shape=jax.ShapeDtypeStruct((8, TILES + 1, K, 128), bf16),
        compiler_params=params,
        name="fold",
    )(pieces)
    pieces = exchange(pieces, Z)
    return pl.pallas_call(
        finish_kernel,
        in_specs=[vmem],
        out_specs=vmem,
        out_shape=jax.ShapeDtypeStruct((K, TILES * 128), f32),
        compiler_params=params,
        name="finish",
    )(pieces)


def on_device(particles, shift_index, prev_class, prev_rotation, precision, references):
    own, other, shifted = gather_table(references, particles, shift_index)
    scores, stats, images = local_scores(own, other, shifted, prev_class, prev_rotation, precision)
    stats = exchange(stats, CLS)
    keep, send, evidence = local_sums(stats, scores, images)
    return (scatter_sums(keep, send), evidence)


def solution(mesh):
    split = Mesh(mesh.devices.reshape(4, 2, 4, 2, 2, 4), DOM + CLS)
    return jax.shard_map(
        on_device,
        mesh=split,
        in_specs=(P(DOM, None), P(DOM), P(DOM), P(DOM), P(DOM), P(CLS, DOM)),
        out_specs=(P(CLS, DOM), P(DOM)),
        check_vma=False,
    )
```

```python
import math

import jax
import jax.numpy as jnp
import ml_dtypes
import numpy as np
from jax import lax
from jax.experimental import pallas as pl
from jax.experimental.pallas import tpu as pltpu
from jax.sharding import Mesh
from jax.sharding import PartitionSpec as P

BOX = 64
F = 4096
H = F // 2
R = 24
K = 8
ROWS = K * R
SHIFTS = 25
SIDE = 5
P_DEV = 576
ROW_BLOCK = 288
TILES = 12
PIECES = 96

bf16 = jnp.bfloat16
f32 = jnp.float32

Z = ("za", "zb")
CLS = ("zh", "x")
DOM = ("y", "za", "zb", "c")


def phase_table():
    frequency = np.arange(H)
    shift = np.arange(SHIFTS)
    step_x, step_y = shift % SIDE - 2, shift // SIDE - 2
    phase = (np.outer(step_x, frequency % BOX - BOX // 2) + np.outer(step_y, frequency // BOX)) % BOX
    angle = phase * (2.0 * math.pi / BOX)
    rest = np.concatenate([np.cos(angle), np.sin(angle)], axis=1).astype(np.float32)
    terms = []
    for _ in range(3):
        terms.append(rest.astype(ml_dtypes.bfloat16))
        rest = rest - terms[-1].astype(np.float32)
    terms.append(np.zeros((128 - 3 * SHIFTS, F), ml_dtypes.bfloat16))
    return jnp.asarray(np.concatenate(terms, axis=0))


def shift_kernel(index_ref, table_ref, image_ref, out_ref):
    index = index_ref[...]
    lane = lax.broadcasted_iota(jnp.int32, (ROW_BLOCK, 128), 1)
    chosen = (lane == index) | (lane == index + SHIFTS) | (lane == index + 2 * SHIFTS)
    chosen = jnp.where(chosen, 1.0, 0.0).astype(bf16)
    for at in range(0, H, 512):
        cosine = jnp.dot(chosen, table_ref[:, at : at + 512], preferred_element_type=f32)
        sine = jnp.dot(chosen, table_ref[:, H + at : H + at + 512], preferred_element_type=f32)
        real = image_ref[:, at : at + 512].astype(f32)
        imag = image_ref[:, H + at : H + at + 512].astype(f32)
        out_ref[:, at : at + 512] = (real * cosine + imag * sine).astype(bf16)
        out_ref[:, H + at : H + at + 512] = (imag * cosine - real * sine).astype(bf16)


def shift_particles(particles, shift_index, table):
    return pl.pallas_call(
        shift_kernel,
        grid=(P_DEV // ROW_BLOCK,),
        in_specs=[
            pl.BlockSpec((ROW_BLOCK, 1), lambda i: (i, 0)),
            pl.BlockSpec((128, F), lambda i: (0, 0)),
            pl.BlockSpec((ROW_BLOCK, F), lambda i: (i, 0)),
        ],
        out_specs=pl.BlockSpec((ROW_BLOCK, F), lambda i: (i, 0)),
        out_shape=pltpu.HBM((P_DEV, F), bf16),
        compiler_params=pltpu.CompilerParams(vmem_limit_bytes=16 << 20),
        name="shift",
    )(shift_index, table, pltpu.with_memory_space_constraint(particles, pltpu.HBM))


def exchange(array, axis):
    return lax.all_to_all(array, axis, 0, 0, tiled=True)


def gather_table(references, particles, shift_index):
    mine = references.reshape(K, TILES, 128).transpose(1, 0, 2)
    along_z = exchange(jnp.broadcast_to(mine, (8, TILES, K, 128)), Z)
    shifted = shift_particles(particles, shift_index[:, None], phase_table())
    along_z, shifted = lax.optimization_barrier((along_z, shifted))
    along_y = exchange(jnp.broadcast_to(along_z, (4, 8, TILES, K, 128)), "y")
    other = lax.ppermute(along_y, "c", [(0, 1), (1, 0)])
    return along_y.reshape(8, 4, TILES, K, 128), other.reshape(8, 4, TILES, K, 128), shifted


def fill_table(source_ref, table_ref, core):
    for zb in range(4):
        for b in range(3):
            part = 6 * zb + 3 * core + b
            turn = part // 8
            column = (part - 8 * turn) * 512
            rows = pl.ds(pl.multiple_of(turn * 64, 64), 64)
            for lanes in range(4):
                tiles = source_ref[:, zb, 4 * b + lanes].reshape(64, 128)
                table_ref[rows, pl.ds(pl.multiple_of(column + lanes * 128, 128), 128)] = tiles


def load_kernel(own_ref, shifted_ref, images_ref, table_ref, arrived):
    copies = []
    for q in range(8):
        columns = pl.ds(q * 512, 512)
        copies.append(pltpu.make_async_copy(shifted_ref.at[:, columns], images_ref.at[:, columns], arrived.at[q]))
        copies[-1].start()
    fill_table(own_ref, table_ref, lax.axis_index("c"))
    for copy in copies:
        copy.wait()


def load_own(own, shifted):
    vmem = pl.BlockSpec(memory_space=pltpu.VMEM)
    return pl.pallas_call(
        load_kernel,
        in_specs=[vmem, pl.BlockSpec(memory_space=pltpu.HBM)],
        out_specs=[vmem, vmem],
        out_shape=[pltpu.VMEM((P_DEV, F), bf16), pltpu.VMEM((ROWS, F), bf16)],
        scratch_shapes=[pltpu.SemaphoreType.DMA((8,))],
        compiler_params=pltpu.CompilerParams(vmem_limit_bytes=16 << 20),
        name="load",
    )(own, pltpu.with_memory_space_constraint(shifted, pltpu.HBM))


def score_kernel(other_ref, half_ref, shifted_ref, class_ref, rotation_ref, precision_ref, scores_ref, stats_ref, table_ref):
    fill_table(other_ref, table_ref, 1 - lax.axis_index("c"))
    half_norm = jnp.zeros((ROWS, 128), f32)
    for at in range(0, F, 128):
        piece = table_ref[:, at : at + 128].astype(f32)
        half_norm = half_norm + piece * piece
    half_norm = 0.5 * jnp.sum(half_norm, axis=1, keepdims=True)
    correlation = lax.dot_general(shifted_ref[...], table_ref[...], (((1,), (1,)), ((), ())), preferred_element_type=f32).T
    row = lax.broadcasted_iota(jnp.int32, (ROWS, 1), 0)
    class_ids = lax.axis_index(CLS) * K + row % K
    rotation_ids = (row // K) % 8 * 3 + row // 64
    distance = jnp.abs(rotation_ids - rotation_ref[...])
    distance = jnp.minimum(distance, R - distance).astype(f32)
    width = R / 8.0
    match = jnp.where(class_ids == class_ref[...], 1.0, 0.0)
    scores = precision_ref[...] * (correlation - half_norm) + (-distance * distance / (2.0 * width * width) + match)
    scores_ref[...] = scores
    top = jnp.max(scores, axis=0, keepdims=True)
    mass = jnp.sum(jnp.exp(scores - top), axis=0, keepdims=True)
    for at in range(8):
        stats_ref[at, 0:1, :] = top
        stats_ref[at, 1:2, :] = mass


def local_scores(own, other, shifted, prev_class, prev_rotation, precision):
    images, half = load_own(own, shifted)
    vmem = pl.BlockSpec(memory_space=pltpu.VMEM)
    scores, stats, _ = pl.pallas_call(
        score_kernel,
        in_specs=[vmem] * 6,
        out_specs=[vmem, vmem, vmem],
        out_shape=[jax.ShapeDtypeStruct((ROWS, P_DEV), f32), jax.ShapeDtypeStruct((8, 2, P_DEV), f32), pltpu.VMEM((ROWS, F), bf16)],
        input_output_aliases={1: 2},
        compiler_params=pltpu.CompilerParams(vmem_limit_bytes=16 << 20),
        name="scores",
    )(other, half, images, prev_class[None, :], prev_rotation[None, :], precision[None, :])
    return scores, stats, images


def sum_kernel(stats_ref, scores_ref, shifted_ref, keep_ref, send_ref, evidence_ref):
    tops = [stats_ref[i, 0:1, :] for i in range(8)]
    top = tops[0]
    for i in range(1, 8):
        top = jnp.maximum(top, tops[i])
    mass = jnp.zeros_like(top)
    for i in range(8):
        mass = mass + stats_ref[i, 1:2, :] * jnp.exp(tops[i] - top)
    evidence_ref[...] = (top + jnp.log(mass)).reshape(P_DEV)
    probs = jnp.exp(scores_ref[...] - top) * (1.0 / mass)
    weights = probs.astype(bf16)
    occupancy = jnp.sum(probs, axis=1, keepdims=True)
    high = occupancy.astype(bf16).astype(f32)
    low = occupancy - high
    lane = lax.broadcasted_iota(jnp.int32, (4, K, 128), 2)
    masses = [jnp.zeros((4, K, 128), f32), jnp.zeros((4, K, 128), f32)]
    for za in range(2):
        for turn in range(3):
            rows = slice(64 * turn, 64 * turn + 64)
            spread_high = jnp.broadcast_to(high[rows].reshape(4, 2, K, 1)[:, za], (4, K, 128))
            spread_low = jnp.broadcast_to(low[rows].reshape(4, 2, K, 1)[:, za], (4, K, 128))
            for part in range(8 * turn, 8 * turn + 8):
                zb, to, b = part // 6, part // 3 % 2, part % 3
                at = 6 * (4 * za + zb) + b
                masses[to] = jnp.where(lane == at, spread_high, masses[to])
                masses[to] = jnp.where(lane == at + 3, spread_low, masses[to])

    swap = lax.axis_index("c") == 1
    numerators = {}
    for q in range(8):
        numerator = jnp.dot(weights, shifted_ref[:, q * 512 : q * 512 + 512], preferred_element_type=f32)
        for turn in range(3):
            numerators[8 * turn + q] = numerator[64 * turn : 64 * turn + 64]
    for part in range(24):
        if part // 3 % 2:
            continue
        zb, b = part // 6, part % 3
        first, second = numerators[part], numerators[part + 3]
        keep = jnp.where(swap, second, first)
        send = jnp.where(swap, first, second)
        for lanes in range(4):
            columns = slice(128 * lanes, 128 * lanes + 128)
            for za in range(2):
                at = 12 * (4 * za + zb) + 4 * b + lanes
                keep_ref[:, at] = keep[:, columns].reshape(4, 2, K, 128)[:, za]
                send_ref[:, at] = send[:, columns].reshape(4, 2, K, 128)[:, za].astype(bf16)
    keep_ref[:, PIECES] = jnp.where(swap, masses[1], masses[0])
    send_ref[:, PIECES] = jnp.where(swap, masses[0], masses[1]).astype(bf16)


def local_sums(stats, scores, shifted):
    vmem = pl.BlockSpec(memory_space=pltpu.VMEM)
    return pl.pallas_call(
        sum_kernel,
        in_specs=[vmem] * 3,
        out_specs=[vmem, vmem, vmem],
        out_shape=[
            jax.ShapeDtypeStruct((4, PIECES + 1, K, 128), f32),
            jax.ShapeDtypeStruct((4, PIECES + 1, K, 128), bf16),
            jax.ShapeDtypeStruct((P_DEV,), f32),
        ],
        compiler_params=pltpu.CompilerParams(vmem_limit_bytes=16 << 20),
        name="sums",
    )(stats, scores, shifted)


def fold_kernel(pieces_ref, out_ref):
    total = pieces_ref[0].astype(f32)
    for i in range(1, 4):
        total = total + pieces_ref[i].astype(f32)
    total = total.astype(bf16)
    for i in range(8):
        out_ref[i, 0:TILES] = total[TILES * i : TILES * i + TILES]
        out_ref[i, TILES] = total[PIECES]


def finish_kernel(pieces_ref, out_ref):
    total = pieces_ref[0].astype(f32)
    for i in range(1, 8):
        total = total + pieces_ref[i].astype(f32)
    lane = lax.broadcasted_iota(jnp.int32, (K, 128), 1) - 6 * lax.axis_index(Z)
    for b in range(3):
        picked = jnp.where((lane == b) | (lane == b + 3), total[TILES], 0.0)
        scale = 1.0 / (jnp.sum(picked, axis=1, keepdims=True) + 1.0)
        for lanes in range(4):
            at = 4 * b + lanes
            out_ref[:, at * 128 : at * 128 + 128] = total[at] * scale


def scatter_sums(keep, send):
    vmem = pl.BlockSpec(memory_space=pltpu.VMEM)
    params = pltpu.CompilerParams(vmem_limit_bytes=16 << 20)
    received = lax.ppermute(send, "c", [(0, 1), (1, 0)])
    pieces = exchange((keep + received.astype(f32)).astype(bf16), "y")
    pieces = pl.pallas_call(
        fold_kernel,
        in_specs=[vmem],
        out_specs=vmem,
        out_shape=jax.ShapeDtypeStruct((8, TILES + 1, K, 128), bf16),
        compiler_params=params,
        name="fold",
    )(pieces)
    pieces = exchange(pieces, Z)
    return pl.pallas_call(
        finish_kernel,
        in_specs=[vmem],
        out_specs=vmem,
        out_shape=jax.ShapeDtypeStruct((K, TILES * 128), f32),
        compiler_params=params,
        name="finish",
    )(pieces)


def on_device(particles, shift_index, prev_class, prev_rotation, precision, references):
    own, other, shifted = gather_table(references, particles, shift_index)
    scores, stats, images = local_scores(own, other, shifted, prev_class, prev_rotation, precision)
    stats = exchange(stats, CLS)
    keep, send, evidence = local_sums(stats, scores, images)
    return (scatter_sums(keep, send), evidence)


def solution(mesh):
    split = Mesh(mesh.devices.reshape(4, 2, 4, 2, 2, 4), DOM + CLS)
    return jax.shard_map(
        on_device,
        mesh=split,
        in_specs=(P(DOM, None), P(DOM), P(DOM), P(DOM), P(DOM), P(CLS, DOM)),
        out_specs=(P(CLS, DOM), P(DOM)),
        check_vma=False,
    )
```

```python
import math

import jax
import jax.numpy as jnp
import ml_dtypes
import numpy as np
from jax import lax
from jax.experimental import pallas as pl
from jax.experimental.pallas import tpu as pltpu
from jax.sharding import Mesh
from jax.sharding import PartitionSpec as P

BOX = 64
F = 4096
H = F // 2
R = 24
K = 8
ROWS = K * R
SHIFTS = 25
SIDE = 5
P_DEV = 576
ROW_BLOCK = 288
TILES = 12
PIECES = 96

bf16 = jnp.bfloat16
f32 = jnp.float32

Z = ("za", "zb")
CLS = ("zh", "x")
DOM = ("y", "za", "zb", "c")


def phase_table():
    frequency = np.arange(H)
    shift = np.arange(SHIFTS)
    step_x, step_y = shift % SIDE - 2, shift // SIDE - 2
    phase = (np.outer(step_x, frequency % BOX - BOX // 2) + np.outer(step_y, frequency // BOX)) % BOX
    angle = phase * (2.0 * math.pi / BOX)
    rest = np.concatenate([np.cos(angle), np.sin(angle)], axis=1).astype(np.float32)
    terms = []
    for _ in range(3):
        terms.append(rest.astype(ml_dtypes.bfloat16))
        rest = rest - terms[-1].astype(np.float32)
    terms.append(np.zeros((128 - 3 * SHIFTS, F), ml_dtypes.bfloat16))
    return jnp.asarray(np.concatenate(terms, axis=0))


def shift_kernel(index_ref, table_ref, image_ref, out_ref):
    index = index_ref[...]
    lane = lax.broadcasted_iota(jnp.int32, (ROW_BLOCK, 128), 1)
    chosen = (lane == index) | (lane == index + SHIFTS) | (lane == index + 2 * SHIFTS)
    chosen = jnp.where(chosen, 1.0, 0.0).astype(bf16)
    for at in range(0, H, 512):
        cosine = jnp.dot(chosen, table_ref[:, at : at + 512], preferred_element_type=f32)
        sine = jnp.dot(chosen, table_ref[:, H + at : H + at + 512], preferred_element_type=f32)
        real = image_ref[:, at : at + 512].astype(f32)
        imag = image_ref[:, H + at : H + at + 512].astype(f32)
        out_ref[:, at : at + 512] = (real * cosine + imag * sine).astype(bf16)
        out_ref[:, H + at : H + at + 512] = (imag * cosine - real * sine).astype(bf16)


def shift_particles(particles, shift_index, table):
    return pl.pallas_call(
        shift_kernel,
        grid=(P_DEV // ROW_BLOCK,),
        in_specs=[
            pl.BlockSpec((ROW_BLOCK, 1), lambda i: (i, 0)),
            pl.BlockSpec((128, F), lambda i: (0, 0)),
            pl.BlockSpec((ROW_BLOCK, F), lambda i: (i, 0)),
        ],
        out_specs=pl.BlockSpec((ROW_BLOCK, F), lambda i: (i, 0)),
        out_shape=pltpu.HBM((P_DEV, F), bf16),
        compiler_params=pltpu.CompilerParams(vmem_limit_bytes=16 << 20),
        name="shift",
    )(shift_index, table, pltpu.with_memory_space_constraint(particles, pltpu.HBM))


def exchange(array, axis):
    return lax.all_to_all(array, axis, 0, 0, tiled=True)


def gather_table(references, particles, shift_index):
    mine = references.reshape(K, TILES, 128).transpose(1, 0, 2)
    along_z = exchange(jnp.broadcast_to(mine, (8, TILES, K, 128)), Z)
    along_z, index = lax.optimization_barrier((along_z, shift_index))
    along_y = exchange(jnp.broadcast_to(along_z, (4, 8, TILES, K, 128)), "y")
    along_y, shifted = lax.optimization_barrier((along_y, shift_particles(particles, index[:, None], phase_table())))
    other = lax.ppermute(along_y, "c", [(0, 1), (1, 0)])
    return along_y.reshape(8, 4, TILES, K, 128), other.reshape(8, 4, TILES, K, 128), shifted


def fill_table(source_ref, table_ref, core):
    for zb in range(4):
        for b in range(3):
            part = 6 * zb + 3 * core + b
            turn = part // 8
            column = (part - 8 * turn) * 512
            rows = pl.ds(pl.multiple_of(turn * 64, 64), 64)
            for lanes in range(4):
                tiles = source_ref[:, zb, 4 * b + lanes].reshape(64, 128)
                table_ref[rows, pl.ds(pl.multiple_of(column + lanes * 128, 128), 128)] = tiles


def load_kernel(own_ref, shifted_ref, images_ref, table_ref, arrived):
    copies = []
    for q in range(8):
        columns = pl.ds(q * 512, 512)
        copies.append(pltpu.make_async_copy(shifted_ref.at[:, columns], images_ref.at[:, columns], arrived.at[q]))
        copies[-1].start()
    fill_table(own_ref, table_ref, lax.axis_index("c"))
    for copy in copies:
        copy.wait()


def load_own(own, shifted):
    vmem = pl.BlockSpec(memory_space=pltpu.VMEM)
    return pl.pallas_call(
        load_kernel,
        in_specs=[vmem, pl.BlockSpec(memory_space=pltpu.HBM)],
        out_specs=[vmem, vmem],
        out_shape=[pltpu.VMEM((P_DEV, F), bf16), pltpu.VMEM((ROWS, F), bf16)],
        scratch_shapes=[pltpu.SemaphoreType.DMA((8,))],
        compiler_params=pltpu.CompilerParams(vmem_limit_bytes=16 << 20),
        name="load",
    )(own, pltpu.with_memory_space_constraint(shifted, pltpu.HBM))


def score_kernel(other_ref, half_ref, shifted_ref, class_ref, rotation_ref, precision_ref, scores_ref, stats_ref, table_ref):
    fill_table(other_ref, table_ref, 1 - lax.axis_index("c"))
    half_norm = jnp.zeros((ROWS, 128), f32)
    for at in range(0, F, 128):
        piece = table_ref[:, at : at + 128].astype(f32)
        half_norm = half_norm + piece * piece
    half_norm = 0.5 * jnp.sum(half_norm, axis=1, keepdims=True)
    correlation = lax.dot_general(shifted_ref[...], table_ref[...], (((1,), (1,)), ((), ())), preferred_element_type=f32).T
    row = lax.broadcasted_iota(jnp.int32, (ROWS, 1), 0)
    class_ids = lax.axis_index(CLS) * K + row % K
    rotation_ids = (row // K) % 8 * 3 + row // 64
    distance = jnp.abs(rotation_ids - rotation_ref[...])
    distance = jnp.minimum(distance, R - distance).astype(f32)
    width = R / 8.0
    match = jnp.where(class_ids == class_ref[...], 1.0, 0.0)
    scores = precision_ref[...] * (correlation - half_norm) + (-distance * distance / (2.0 * width * width) + match)
    scores_ref[...] = scores
    top = jnp.max(scores, axis=0, keepdims=True)
    mass = jnp.sum(jnp.exp(scores - top), axis=0, keepdims=True)
    for at in range(8):
        stats_ref[at, 0:1, :] = top
        stats_ref[at, 1:2, :] = mass


def local_scores(own, other, shifted, prev_class, prev_rotation, precision):
    images, half = load_own(own, shifted)
    vmem = pl.BlockSpec(memory_space=pltpu.VMEM)
    scores, stats, _ = pl.pallas_call(
        score_kernel,
        in_specs=[vmem] * 6,
        out_specs=[vmem, vmem, vmem],
        out_shape=[jax.ShapeDtypeStruct((ROWS, P_DEV), f32), jax.ShapeDtypeStruct((8, 2, P_DEV), f32), pltpu.VMEM((ROWS, F), bf16)],
        input_output_aliases={1: 2},
        compiler_params=pltpu.CompilerParams(vmem_limit_bytes=16 << 20),
        name="scores",
    )(other, half, images, prev_class[None, :], prev_rotation[None, :], precision[None, :])
    return scores, stats, images


def sum_kernel(stats_ref, scores_ref, shifted_ref, keep_ref, send_ref, evidence_ref):
    tops = [stats_ref[i, 0:1, :] for i in range(8)]
    top = tops[0]
    for i in range(1, 8):
        top = jnp.maximum(top, tops[i])
    mass = jnp.zeros_like(top)
    for i in range(8):
        mass = mass + stats_ref[i, 1:2, :] * jnp.exp(tops[i] - top)
    evidence_ref[...] = (top + jnp.log(mass)).reshape(P_DEV)
    probs = jnp.exp(scores_ref[...] - top) * (1.0 / mass)
    weights = probs.astype(bf16)
    occupancy = jnp.sum(probs, axis=1, keepdims=True)
    high = occupancy.astype(bf16).astype(f32)
    low = occupancy - high
    lane = lax.broadcasted_iota(jnp.int32, (4, K, 128), 2)
    masses = [jnp.zeros((4, K, 128), f32), jnp.zeros((4, K, 128), f32)]
    for za in range(2):
        for turn in range(3):
            rows = slice(64 * turn, 64 * turn + 64)
            spread_high = jnp.broadcast_to(high[rows].reshape(4, 2, K, 1)[:, za], (4, K, 128))
            spread_low = jnp.broadcast_to(low[rows].reshape(4, 2, K, 1)[:, za], (4, K, 128))
            for part in range(8 * turn, 8 * turn + 8):
                zb, to, b = part // 6, part // 3 % 2, part % 3
                at = 6 * (4 * za + zb) + b
                masses[to] = jnp.where(lane == at, spread_high, masses[to])
                masses[to] = jnp.where(lane == at + 3, spread_low, masses[to])

    swap = lax.axis_index("c") == 1
    numerators = {}
    for q in range(8):
        numerator = jnp.dot(weights, shifted_ref[:, q * 512 : q * 512 + 512], preferred_element_type=f32)
        for turn in range(3):
            numerators[8 * turn + q] = numerator[64 * turn : 64 * turn + 64]
    for part in range(24):
        if part // 3 % 2:
            continue
        zb, b = part // 6, part % 3
        first, second = numerators[part], numerators[part + 3]
        keep = jnp.where(swap, second, first)
        send = jnp.where(swap, first, second)
        for lanes in range(4):
            columns = slice(128 * lanes, 128 * lanes + 128)
            for za in range(2):
                at = 12 * (4 * za + zb) + 4 * b + lanes
                keep_ref[:, at] = keep[:, columns].reshape(4, 2, K, 128)[:, za]
                send_ref[:, at] = send[:, columns].reshape(4, 2, K, 128)[:, za].astype(bf16)
    keep_ref[:, PIECES] = jnp.where(swap, masses[1], masses[0])
    send_ref[:, PIECES] = jnp.where(swap, masses[0], masses[1]).astype(bf16)


def local_sums(stats, scores, shifted):
    vmem = pl.BlockSpec(memory_space=pltpu.VMEM)
    return pl.pallas_call(
        sum_kernel,
        in_specs=[vmem] * 3,
        out_specs=[vmem, vmem, vmem],
        out_shape=[
            jax.ShapeDtypeStruct((4, PIECES + 1, K, 128), f32),
            jax.ShapeDtypeStruct((4, PIECES + 1, K, 128), bf16),
            jax.ShapeDtypeStruct((P_DEV,), f32),
        ],
        compiler_params=pltpu.CompilerParams(vmem_limit_bytes=16 << 20),
        name="sums",
    )(stats, scores, shifted)


def fold_kernel(pieces_ref, out_ref):
    total = pieces_ref[0].astype(f32)
    for i in range(1, 4):
        total = total + pieces_ref[i].astype(f32)
    total = total.astype(bf16)
    for i in range(8):
        out_ref[i, 0:TILES] = total[TILES * i : TILES * i + TILES]
        out_ref[i, TILES] = total[PIECES]


def finish_kernel(pieces_ref, out_ref):
    total = pieces_ref[0].astype(f32)
    for i in range(1, 8):
        total = total + pieces_ref[i].astype(f32)
    lane = lax.broadcasted_iota(jnp.int32, (K, 128), 1) - 6 * lax.axis_index(Z)
    for b in range(3):
        picked = jnp.where((lane == b) | (lane == b + 3), total[TILES], 0.0)
        scale = 1.0 / (jnp.sum(picked, axis=1, keepdims=True) + 1.0)
        for lanes in range(4):
            at = 4 * b + lanes
            out_ref[:, at * 128 : at * 128 + 128] = total[at] * scale


def scatter_sums(keep, send):
    vmem = pl.BlockSpec(memory_space=pltpu.VMEM)
    params = pltpu.CompilerParams(vmem_limit_bytes=16 << 20)
    received = lax.ppermute(send, "c", [(0, 1), (1, 0)])
    pieces = exchange((keep + received.astype(f32)).astype(bf16), "y")
    pieces = pl.pallas_call(
        fold_kernel,
        in_specs=[vmem],
        out_specs=vmem,
        out_shape=jax.ShapeDtypeStruct((8, TILES + 1, K, 128), bf16),
        compiler_params=params,
        name="fold",
    )(pieces)
    pieces = exchange(pieces, Z)
    return pl.pallas_call(
        finish_kernel,
        in_specs=[vmem],
        out_specs=vmem,
        out_shape=jax.ShapeDtypeStruct((K, TILES * 128), f32),
        compiler_params=params,
        name="finish",
    )(pieces)


def on_device(particles, shift_index, prev_class, prev_rotation, precision, references):
    own, other, shifted = gather_table(references, particles, shift_index)
    scores, stats, images = local_scores(own, other, shifted, prev_class, prev_rotation, precision)
    stats = exchange(stats, CLS)
    keep, send, evidence = local_sums(stats, scores, images)
    return (scatter_sums(keep, send), evidence)


def solution(mesh):
    split = Mesh(mesh.devices.reshape(4, 2, 4, 2, 2, 4), DOM + CLS)
    return jax.shard_map(
        on_device,
        mesh=split,
        in_specs=(P(DOM, None), P(DOM), P(DOM), P(DOM), P(DOM), P(CLS, DOM)),
        out_specs=(P(CLS, DOM), P(DOM)),
        check_vma=False,
    )
```
